256 devices in a mesh: gx: 8 (over z), gy: 32 (over x, y, core).
Axes of the slice: x: 4, y: 4, z: 8, core: 2. Of those that a mesh axis runs over, the one named last changes fastest.
Arguments:
- right_side: float32 [256, 1024, 128], P('gx', 'gy'), may hold values from -6 to 6
- permittivity: float32 [256, 1024, 128], P('gx', 'gy'), may hold values from 0.175 to 5.6
Outputs:
- potential: float32 [256, 1024, 128], P('gx', 'gy')
The draws below stay inside these ranges and needn't reach their ends.
All inputs are finite; a program needn't handle non-finite values.
Results may differ from the reference program's by a relative error of at most 0.00002.
Values sent between devices are 32-bit elements; how exact they have to be, the bound alone decides.
No kernel may reach another device: no remote copies, remote signals or barrier semaphores. Data moves between devices by JAX's collectives and lax.ppermute only.
A program may use at most 192 MiB of HBM per device.

```python
import jax
import jax.numpy as jnp

LEVELS = 5
SMOOTH = 2
COARSE_SWEEPS = 12
NX = 256
NY = 1024
NZ = 128


def draw_right_side(key, part):
    grid_shape = (NX, NY, NZ)
    return jnp.clip(0.75 + jax.random.normal(key, grid_shape, jnp.float32), -6.0, 6.0)


def draw_permittivity(key, part):
    grid_shape = (NX, NY, NZ)
    block_cells = 2 ** (LEVELS - 1)
    index_x = jnp.arange(NX, dtype=jnp.int32) // block_cells
    index_z = jnp.arange(NZ, dtype=jnp.int32) // block_cells
    fibre_on = (index_x[:, None, None] + index_z[None, None, :]) % 2 == 0
    background = jnp.where(fibre_on, jnp.float32(4.0), jnp.float32(0.25))
    factor = jnp.exp(jax.random.uniform(key, grid_shape, jnp.float32, jnp.log(0.7), jnp.log(1.4)))
    return jnp.broadcast_to(background, grid_shape) * factor


def setup_inputs(seed: int = 0) -> dict:
    streams_of = jax.random.split(jax.random.key(seed), 3)
    right_side = draw_right_side(jax.random.fold_in(streams_of[2], 71), 0)
    permittivity = draw_permittivity(jax.random.fold_in(streams_of[2], 71), 0)
    return {"right_side": right_side, "permittivity": permittivity}


def restrict(values):
    rows_x, rows_y, rows_z = values.shape
    return values.reshape(rows_x // 2, 2, rows_y // 2, 2, rows_z // 2, 2).sum(axis=(1, 3, 5)) * 0.125


def inject(values):
    rows_x, rows_y, rows_z = values.shape
    spread_out = jnp.broadcast_to(values[:, None, :, None, :, None], (rows_x, 2, rows_y, 2, rows_z, 2))
    return spread_out.reshape(2 * rows_x, 2 * rows_y, 2 * rows_z)


def side_values(extended):
    return (extended[2:, 1:-1, 1:-1], extended[:-2, 1:-1, 1:-1], extended[1:-1, 2:, 1:-1],
            extended[1:-1, :-2, 1:-1], extended[1:-1, 1:-1, 2:], extended[1:-1, 1:-1, :-2])


def face_weights(permit, extended, level_scale):
    return tuple(level_scale * 2.0 * permit * neighbour / (permit + neighbour) for neighbour in side_values(extended))


def beside_sum(weights, extended):
    values = side_values(extended)
    running = weights[0] * values[0]
    for k in range(1, 6):
        running = running + weights[k] * values[k]
    return running


def weight_total(weights):
    running = weights[0]
    for k in range(1, 6):
        running = running + weights[k]
    return running


def colours(rows_x, rows_y, rows_z, offset_x, offset_y):
    index_x = offset_x + jnp.arange(rows_x, dtype=jnp.int32)
    index_y = offset_y + jnp.arange(rows_y, dtype=jnp.int32)
    index_z = jnp.arange(rows_z, dtype=jnp.int32)
    return (index_x[:, None, None] + index_y[None, :, None] + index_z[None, None, :]) % 2


def pad_permit(permit):
    edged = jnp.pad(permit, ((1, 1), (1, 1), (0, 0)), mode="edge")
    return jnp.pad(edged, ((0, 0), (0, 0), (1, 1)))


def smooth(potential, source, weights, weight_sum, parity, sweeps):
    for sweep_index in range(sweeps):
        for colour in range(2):
            updated = (source + beside_sum(weights, jnp.pad(potential, 1))) / weight_sum
            potential = jnp.where(parity == colour, updated, potential)
    return potential


def cycle(level_index, source, permit):
    level_scale = 0.25 ** level_index
    weights = face_weights(permit, pad_permit(permit), level_scale)
    weight_sum = weight_total(weights)
    rows_x, rows_y, rows_z = source.shape
    parity = colours(rows_x, rows_y, rows_z, 0, 0)
    zeros_start = jnp.zeros(source.shape, jnp.float32)
    if level_index == LEVELS - 1:
        return smooth(zeros_start, source, weights, weight_sum, parity, COARSE_SWEEPS)
    potential = smooth(zeros_start, source, weights, weight_sum, parity, SMOOTH)
    residual_field = source - (weight_sum * potential - beside_sum(weights, jnp.pad(potential, 1)))
    correction = cycle(level_index + 1, restrict(residual_field), restrict(permit))
    potential = potential + inject(correction)
    return smooth(potential, source, weights, weight_sum, parity, SMOOTH)


def reference(right_side, permittivity):
    return cycle(0, right_side, permittivity)
```

```python
import jax
import jax.numpy as jnp
from jax import lax
from jax.experimental import pallas as pl
from jax.experimental.pallas import tpu as pltpu
from jax.sharding import PartitionSpec as P

F32 = jnp.float32
LANES = 128
COARSE_SWEEPS = 12
OWN = (32, 16, 8)
HALO = (8, 16, 12)
EXT = (48, 48, 32)
GX = 8
GY = 32
CHUNK = 8


def iota(shape, dim):
    return lax.broadcasted_iota(jnp.int32, shape, dim)


def lane_roll(v, shift):
    return pltpu.roll(v, shift % LANES, v.ndim - 1)


def flip(v, bit):
    lane = iota(v.shape, v.ndim - 1)
    return jnp.where((lane & bit) == 0, lane_roll(v, -bit), lane_roll(v, bit))


def pair_is_even(level, rows):
    shape = (rows, LANES)
    return ((iota(shape, 0) ^ (iota(shape, 1) >> level)) & 1) == 0


def bounds(level, index, count):
    own, halo, ext = OWN[level], HALO[level], EXT[level]
    low = halo - index * own
    high = halo + (count - index) * own
    return low, high


def clamp_edges(level, e, gx, gy):
    own, halo, ext = OWN[level], HALO[level], EXT[level]
    for back in range(-(-halo // own)):
        low = halo - back * own
        high = halo + own + back * own
        if low >= 1:

            @pl.when(gx == back)
            def _():
                e[low - 1] = e[low]

            @pl.when(gy == back)
            def _():
                e[:, 8 + low - 1 : 8 + low, :] = e[:, 8 + low : 8 + low + 1, :]

        if high < ext:

            @pl.when(gx == GX - 1 - back)
            def _():
                e[high] = e[high - 1]

            @pl.when(gy == GY - 1 - back)
            def _():
                e[:, 8 + high : 8 + high + 1, :] = e[:, 8 + high - 1 : 8 + high, :]


def prepare(level, e, f, state, total, v, gx, gy):
    ext = EXT[level]
    step = 1 << level
    scale = 2.0 * 0.25**level
    rows = 16

    def face(a, b):
        return scale * a * b / (a + b)

    xlow, xhigh = bounds(level, gx, GX)
    ylow, yhigh = bounds(level, gy, GY)
    shape = (rows, LANES)
    lane = iota(shape, 1)
    z_last = (lane >> level) == (LANES >> level) - 1
    even = pair_is_even(level, rows)
    x_odd = jnp.where(even, 0, 1)

    def body(p, carry):
        for c in range(ext // rows):
            r = c * rows
            mid = slice(8 + r, 8 + r + rows)
            up = slice(9 + r, 9 + r + rows)
            down = slice(7 + r, 7 + r + rows)
            e0 = e[2 * p, mid, :]
            e1 = e[2 * p + 1, mid, :]
            before = e[jnp.maximum(2 * p - 1, 0), mid, :]
            after = e[2 * p + 2, mid, :]
            inner = face(e0, e1)
            outer0 = face(e0, before)
            outer1 = face(e1, after)
            yp0 = face(e0, e[2 * p, up, :])
            yp1 = face(e1, e[2 * p + 1, up, :])
            ym0 = face(e0, e[2 * p, down, :])
            ym1 = face(e1, e[2 * p + 1, down, :])
            zp0 = jnp.where(z_last, 0.0, face(e0, lane_roll(e0, -step)))
            zp1 = jnp.where(z_last, 0.0, face(e1, lane_roll(e1, -step)))
            zm0 = lane_roll(zp0, step)
            zm1 = lane_roll(zp1, step)
            f0 = f[2 * p, r : r + rows, :]
            f1 = f[2 * p + 1, r : r + rows, :]
            row = r + iota(shape, 0)
            y_ok = (row >= ylow) & (row < yhigh)
            for k in range(2):
                pick = even if k == 0 else jnp.logical_not(even)
                outer = jnp.where(pick, outer0, outer1)
                yp = jnp.where(pick, yp0, yp1)
                ym = jnp.where(pick, ym0, ym1)
                zp = jnp.where(pick, zp0, zp1)
                zm = jnp.where(pick, zm0, zm1)
                weight_sum = inner + outer + yp + ym + zp + zm
                x_at = 2 * p + (x_odd if k == 0 else 1 - x_odd)
                ok = y_ok & (x_at >= xlow) & (x_at < xhigh)
                inverse = jnp.where(ok, 1.0 / weight_sum, 0.0)
                source = jnp.where(pick, f0, f1) * inverse
                parts = (source, inner * inverse, outer * inverse, yp * inverse, ym * inverse,
                         zp * inverse, zm * inverse)
                for i in range(7):
                    state[k, i, p, r : r + rows, :] = parts[i]
                if k == 0:
                    total[p, r : r + rows, :] = weight_sum
                    v[0, p, mid, :] = source
        return carry

    lax.fori_loop(0, ext // 2, body, 0)


def clear(v, ext):
    def body(p, carry):
        for k in range(2):
            v[k, p] = jnp.zeros((ext + 16, LANES), F32)
        return carry

    lax.fori_loop(0, ext // 2, body, 0)


def updated(level, k, p, v, state):
    ext = EXT[level]
    step = 1 << level
    even = pair_is_even(level, ext)
    mid = slice(8, 8 + ext)
    other = 1 - k
    here = v[other, p, mid, :]
    before = v[other, p - 1, mid, :]
    after = v[other, p + 1, mid, :]
    outer = jnp.where(even, before, after) if k == 0 else jnp.where(even, after, before)
    sides = (here, outer, v[other, p, 9 : 9 + ext, :], v[other, p, 7 : 7 + ext, :],
             lane_roll(here, -step), lane_roll(here, step))
    value = state[k, 0, p]
    for i in range(6):
        value = value + state[k, 1 + i, p] * sides[i]
    return value


def half_sweep(level, k, reach, v, state):
    own, halo, ext = OWN[level], HALO[level], EXT[level]
    first = (halo - reach) // 2
    last = (halo + own + reach + 1) // 2

    def body(p, carry):
        v[k, p, 8 : 8 + ext, :] = updated(level, k, p, v, state)
        return carry

    lax.fori_loop(first, last, body, 0)


def restricted(level, first, row, count, v, state, total, e, tmp, store):
    ext = EXT[level]
    step = 1 << level

    def body(q, carry):
        p = first + q
        mid = slice(8, 8 + ext)
        tmp[0, q, 0:ext, :] = (updated(level, 0, p, v, state) - v[0, p, mid, :]) * total[p]
        tmp[1, q, 0:ext, :] = e[2 * p, mid, :] + e[2 * p + 1, mid, :]
        coarse = []
        for i in range(2):
            a = tmp[i, q, pl.ds(row, count, stride=2), :] + tmp[i, q, pl.ds(row + 1, count, stride=2), :]
            coarse.append((a + flip(a, step)) * 0.125)
        store(q, coarse[0], coarse[1])
        return carry

    return body


def interleave(f, e):
    return jnp.where((iota(f.shape, f.ndim - 1) & 1) == 0, f, e)


def split(both):
    low = (iota(both.shape, both.ndim - 1) & 1) == 0
    return jnp.where(low, both, lane_roll(both, 1)), jnp.where(low, lane_roll(both, -1), both)


def fill_rim(e, ext):
    one = jnp.ones((ext + 16, LANES), F32)
    e[ext] = one
    e[ext + 1] = one

    def body(x, carry):
        e[x, 0:8, :] = one[0:8]
        e[x, 8 + ext :, :] = one[0:8]
        return carry

    lax.fori_loop(0, ext, body, 0)


def down0(f_in, e_in, xl, xr, yl, yr, out, state, v, e, f, total, tmp):
    level = 0
    gx, gy = lax.axis_index("gx"), lax.axis_index("gy")
    fill_rim(e, 48)
    for i, (target, own, off) in enumerate(((f, f_in, 0), (e, e_in, 8))):
        target[0:8, off + 8 : off + 40, :] = xl[i]
        target[8:40, off + 8 : off + 40, :] = own[...]
        target[40:48, off + 8 : off + 40, :] = xr[i]
        target[0:48, off : off + 8, :] = yl[i]
        target[0:48, off + 40 : off + 48, :] = yr[i]
    clamp_edges(level, e, gx, gy)
    clear(v, 48)
    prepare(level, e, f, state, total, v, gx, gy)
    half_sweep(level, 1, 6, v, state)
    half_sweep(level, 0, 5, v, state)
    half_sweep(level, 1, 4, v, state)

    def store(q, fc, ec):
        out[q] = interleave(fc, ec)

    lax.fori_loop(0, 16, restricted(level, 4, 8, 16, v, state, total, e, tmp, store), 0)


def down1(own, xl, xr, yl, yr, out, state, v, e, f, total, tmp):
    level = 1
    gx, gy = lax.axis_index("gx"), lax.axis_index("gy")
    fill_rim(e, 48)

    def put(source, count, x, y):
        def body(i, carry):
            fi, ei = split(source[i])
            f[x + i, y : y + 16, :] = fi
            e[x + i, 8 + y : 8 + y + 16, :] = ei
            return carry

        lax.fori_loop(0, count, body, 0)

    put(xl, 16, 0, 16)
    put(own, 16, 16, 16)
    put(xr, 16, 32, 16)
    put(yl, 48, 0, 0)
    put(yr, 48, 0, 32)
    clamp_edges(level, e, gx, gy)
    clear(v, 48)
    prepare(level, e, f, state, total, v, gx, gy)
    half_sweep(level, 1, 11, v, state)
    half_sweep(level, 0, 10, v, state)
    half_sweep(level, 1, 9, v, state)

    def store(q, fc, ec):
        out[q] = interleave(fc, ec)

    lax.fori_loop(0, 16, restricted(level, 4, 8, 16, v, state, total, e, tmp, store), 0)


def down2(own, xl, xr, yl, yr, out, state, v, e, f, total, tmp, coarse):
    level = 2
    gx, gy = lax.axis_index("gx"), lax.axis_index("gy")
    fill_rim(e, 32)

    def put(source, count, x, y, height):
        def body(i, carry):
            fi, ei = split(source[i])
            f[x + i, y : y + height, :] = fi
            e[x + i, 8 + y : 8 + y + height, :] = ei
            return carry

        lax.fori_loop(0, count, body, 0)

    put(xl, 8, 0, 8, 16)
    put(own, 16, 8, 8, 16)
    put(xr, 8, 24, 8, 16)
    put(yl, 32, 0, 0, 8)
    put(yr, 32, 0, 24, 8)
    clamp_edges(level, e, gx, gy)
    clear(v, 32)
    prepare(level, e, f, state, total, v, gx, gy)
    half_sweep(level, 1, 9, v, state)
    half_sweep(level, 0, 8, v, state)
    half_sweep(level, 1, 7, v, state)

    def store(q, fc, ec):
        coarse[0, q, 0:4, :] = fc
        coarse[1, q, 0:4, :] = ec

    lax.fori_loop(0, 4, restricted(level, 6, 12, 4, v, state, total, e, tmp, store), 0)
    slot = iota((1, LANES), 1) & 7
    for i in range(2):
        for r in range(2):
            row = jnp.zeros((1, LANES), F32)
            for x1 in range(2):
                for y in range(4):
                    row = jnp.where(slot == 4 * x1 + y, coarse[i, 2 * x1 + r, y : y + 1, :], row)
            out[:, 2 * i + r : 2 * i + r + 1, :] = jnp.broadcast_to(row[None], (GX, 1, LANES))


BLOCK = (CHUNK, GX, LANES)


def pair_before(v, fill):
    lane, sub = iota(BLOCK, 2), iota(BLOCK, 1)
    low = (lane & 4) == 0
    moved = jnp.where(low, pltpu.roll(lane_roll(v, -4), 1, 1), lane_roll(v, 4))
    return jnp.where(low & (sub == 0), fill, moved)


def pair_after(v, fill):
    lane, sub = iota(BLOCK, 2), iota(BLOCK, 1)
    high = (lane & 4) != 0
    moved = jnp.where(high, pltpu.roll(lane_roll(v, 4), GX - 1, 1), lane_roll(v, -4))
    return jnp.where(high & (sub == GX - 1), fill, moved)


def y_after(level, v, following):
    lane = iota(BLOCK, 2)
    if level == 3:
        return jnp.where((lane & 3) == 3, lane_roll(following, 3), lane_roll(v, -1))
    return jnp.where((lane & 2) == 2, lane_roll(following, 2), lane_roll(v, -2))


def y_before(level, v, preceding):
    lane = iota(BLOCK, 2)
    if level == 3:
        return jnp.where((lane & 3) == 0, lane_roll(preceding, -3), lane_roll(v, 1))
    return jnp.where((lane & 2) == 0, lane_roll(preceding, -2), lane_roll(v, 2))


def coarse_levels(gathered, e3, s3, w3, v3, e4, f4, s4, v4):
    lane = iota(BLOCK, 2)
    even3 = ((lane ^ (lane >> 3)) & 1) == 0
    even4 = (((lane >> 1) ^ (lane >> 2) ^ (lane >> 4)) & 1) == 0
    z_last3 = (lane >> 3) == 15
    z_last4 = (lane >> 4) == 7
    chunks = range(0, GY, CHUNK)

    def face(scale, a, b):
        return (2.0 * scale) * a * b / (a + b)

    for g in range(GY):
        for r in range(2):
            e3[r, 1 + g] = gathered[g, pl.ds(2 + r, GX, stride=4), :]
    zero = jnp.zeros((GX, LANES), F32)
    for k in range(2):
        e3[k, 0] = lane_roll(e3[k, 1], 3)
        e3[k, 1 + GY] = lane_roll(e3[k, GY], -3)
        v3[k, 0] = zero
        v3[k, 1 + GY] = zero
    v4[0] = zero
    v4[1 + GY] = zero
    scale = 0.25**3
    for g in chunks:
        here = pl.ds(1 + g, CHUNK)
        both = (e3[0, here], e3[1, here])
        inner = face(scale, both[0], both[1])
        outer = (face(scale, both[0], pair_before(both[1], both[0])),
                 face(scale, both[1], pair_after(both[0], both[1])))
        yp, ym, zp, zm, f = [], [], [], [], []
        for r in range(2):
            own = both[r]
            yp.append(face(scale, own, y_after(3, own, e3[r, pl.ds(2 + g, CHUNK)])))
            ym.append(face(scale, own, y_before(3, own, e3[r, pl.ds(g, CHUNK)])))
            z = jnp.where(z_last3, 0.0, face(scale, own, lane_roll(own, -8)))
            zp.append(z)
            zm.append(lane_roll(z, 8))
            f.append(jnp.stack([gathered[g + i, pl.ds(r, GX, stride=4), :] for i in range(CHUNK)]))
        for k in range(2):
            a, b = k, 1 - k
            parts = [jnp.where(even3, t[a], t[b]) for t in (outer, yp, ym, zp, zm)]
            weight_sum = inner
            for t in parts:
                weight_sum = weight_sum + t
            inverse = 1.0 / weight_sum
            source = jnp.where(even3, f[a], f[b]) * inverse
            s3[k, 0, pl.ds(g, CHUNK)] = source
            s3[k, 1, pl.ds(g, CHUNK)] = inner * inverse
            for i in range(5):
                s3[k, 2 + i, pl.ds(g, CHUNK)] = parts[i] * inverse
            if k == 0:
                w3[pl.ds(g, CHUNK)] = weight_sum
                v3[0, here] = source
        t = both[0] + both[1]
        t = t + flip(t, 1)
        e4[here] = (t + flip(t, 8)) * 0.125

    def update3(k, g):
        o = 1 - k
        own = v3[o, pl.ds(1 + g, CHUNK)]
        before, after = pair_before(own, 0.0), pair_after(own, 0.0)
        outer = jnp.where(even3, before, after) if k == 0 else jnp.where(even3, after, before)
        sides = (own, outer, y_after(3, own, v3[o, pl.ds(2 + g, CHUNK)]),
                 y_before(3, own, v3[o, pl.ds(g, CHUNK)]), lane_roll(own, -8), lane_roll(own, 8))
        value = s3[k, 0, pl.ds(g, CHUNK)]
        for i in range(6):
            value = value + s3[k, 1 + i, pl.ds(g, CHUNK)] * sides[i]
        return value

    def sweep3(k):
        for g in chunks:
            v3[k, pl.ds(1 + g, CHUNK)] = update3(k, g)

    sweep3(1)
    sweep3(0)
    sweep3(1)
    for g in chunks:
        t = (update3(0, g) - v3[0, pl.ds(1 + g, CHUNK)]) * w3[pl.ds(g, CHUNK)]
        t = t + flip(t, 1)
        f4[pl.ds(g, CHUNK)] = (t + flip(t, 8)) * 0.125

    e4[0] = lane_roll(e4[1], 2)
    e4[1 + GY] = lane_roll(e4[GY], -2)
    scale = 0.25**4
    for g in chunks:
        own = e4[pl.ds(1 + g, CHUNK)]
        parts = [face(scale, own, pair_before(own, own)), face(scale, own, pair_after(own, own)),
                 face(scale, own, y_after(4, own, e4[pl.ds(2 + g, CHUNK)])),
                 face(scale, own, y_before(4, own, e4[pl.ds(g, CHUNK)]))]
        z = jnp.where(z_last4, 0.0, face(scale, own, lane_roll(own, -16)))
        parts += [z, lane_roll(z, 16)]
        weight_sum = parts[0]
        for t in parts[1:]:
            weight_sum = weight_sum + t
        inverse = 1.0 / weight_sum
        source = f4[pl.ds(g, CHUNK)] * inverse
        s4[0, pl.ds(g, CHUNK)] = source
        for i in range(6):
            s4[1 + i, pl.ds(g, CHUNK)] = parts[i] * inverse
        v4[pl.ds(1 + g, CHUNK)] = jnp.where(even4, source, 0.0)

    def sweep4(k):
        for g in chunks:
            own = v4[pl.ds(1 + g, CHUNK)]
            sides = (pair_before(own, 0.0), pair_after(own, 0.0),
                     y_after(4, own, v4[pl.ds(2 + g, CHUNK)]), y_before(4, own, v4[pl.ds(g, CHUNK)]),
                     lane_roll(own, -16), lane_roll(own, 16))
            value = s4[0, pl.ds(g, CHUNK)]
            for i in range(6):
                value = value + s4[1 + i, pl.ds(g, CHUNK)] * sides[i]
            mine = even4 if k == 0 else jnp.logical_not(even4)
            v4[pl.ds(1 + g, CHUNK)] = jnp.where(mine, value, own)

    sweep4(1)

    def full(i, carry):
        sweep4(0)
        sweep4(1)
        return carry

    lax.fori_loop(0, COARSE_SWEEPS - 1, full, 0)
    for g in chunks:
        here = pl.ds(1 + g, CHUNK)
        u = v4[here]
        v3[0, here] = v3[0, here] + u
        v3[1, here] = v3[1, here] + u
    sweep3(0)
    sweep3(1)
    sweep3(0)
    sweep3(1)


def around_from_level3(v3, up, gx, gy):
    shape = (GX, LANES)
    lane, sub = iota(shape, 1), iota(shape, 0)
    even3 = ((lane ^ (lane >> 3)) & 1) == 0
    head = (lane & 7) == 0
    outside = ((sub == 0) & (gx == 0)) | ((sub == 2) & (gx == GX - 1))
    up[...] = jnp.zeros(up.shape, F32)
    for dy in range(3):
        red = v3[0, gy + dy]
        black = v3[1, gy + dy]
        for r in range(2):
            t = jnp.where(even3, red, black) if r == 0 else jnp.where(even3, black, red)
            t = jnp.where(outside, 0.0, pltpu.roll(t, lax.rem(GX + 1 - gx, GX), 0))
            for s in range(8):
                w = jnp.where(head, lane_roll(t, -s), 0.0)
                w = w + lane_roll(w, 1)
                w = w + lane_roll(w, 2)
                w = w + lane_roll(w, 4)
                for dx in range(3):
                    x = 4 * dx + 2 * (s // 4) + r
                    y = 4 + 2 * (4 * dy + s % 4)
                    up[x, y : y + 2, :] = jnp.broadcast_to(w[dx : dx + 1], (2, LANES))


def spread(level, p, v, up):
    rows = 24
    even = pair_is_even(level, rows)
    start = 8 + (12 if level == 1 else 4)
    red = v[0, p, start : start + rows, :]
    black = v[1, p, start : start + rows, :]
    for s in range(2):
        u = jnp.where(even, red, black) if s == 0 else jnp.where(even, black, red)
        for twice in range(2):
            up[s, pl.ds(twice, rows, stride=2), :] = u


def climb(gathered, s0, in0, s1, in1, s2, in2, out, e3, s3, w3, v3, e4, f4, s4, v4, v2, v1, v0, up3, up):
    gx, gy = lax.axis_index("gx"), lax.axis_index("gy")
    coarse_levels(gathered, e3, s3, w3, v3, e4, f4, s4, v4)
    around_from_level3(v3, up3, gx, gy)

    clear(v2, 32)

    def add2(p, carry):
        for k in range(2):
            v2[k, p, 8:40, :] = in2[k, p, 8:40, :] + up3[p - 2]
        return carry

    lax.fori_loop(2, 14, add2, 0)
    half_sweep(2, 0, 6, v2, s2)
    half_sweep(2, 1, 5, v2, s2)
    half_sweep(2, 0, 4, v2, s2)
    half_sweep(2, 1, 3, v2, s2)

    clear(v1, 48)

    def add1(c, carry):
        slot = up.at[c]
        spread(2, c, v2, slot)
        for s in range(2):
            for k in range(2):
                p = 2 * c - 4 + s
                v1[k, p, 8:56, :] = in1[k, p, 8:56, :] + slot[s]
        return carry

    lax.fori_loop(4, 12, add1, 0)
    half_sweep(1, 0, 5, v1, s1)
    half_sweep(1, 1, 4, v1, s1)
    half_sweep(1, 0, 3, v1, s1)
    half_sweep(1, 1, 2, v1, s1)

    clear(v0, 48)

    def add0(c, carry):
        slot = up.at[c]
        spread(1, c, v1, slot)
        for s in range(2):
            for k in range(2):
                p = 2 * c - 12 + s
                v0[k, p, 8:56, :] = in0[k, p, 8:56, :] + slot[s]
        return carry

    lax.fori_loop(7, 17, add0, 0)
    half_sweep(0, 0, 3, v0, s0)
    half_sweep(0, 1, 2, v0, s0)
    half_sweep(0, 0, 1, v0, s0)
    half_sweep(0, 1, 0, v0, s0)
    even = pair_is_even(0, 32)

    def finish(q, carry):
        red = v0[0, 4 + q, 16:48, :]
        black = v0[1, 4 + q, 16:48, :]
        out[2 * q] = jnp.where(even, red, black)
        out[2 * q + 1] = jnp.where(even, black, red)
        return carry

    lax.fori_loop(0, 16, finish, 0)


def shaped(*dims):
    return jax.ShapeDtypeStruct(dims, F32)


def state_shapes(level):
    ext = EXT[level]
    return shaped(2, 7, ext // 2, ext, LANES), shaped(2, ext // 2, ext + 16, LANES)


def kernel_call(body, out_shape, scratch, *operands):
    return pl.pallas_call(
        body,
        out_shape=out_shape,
        scratch_shapes=[pltpu.VMEM(s, F32) for s in scratch],
        compiler_params=pltpu.CompilerParams(vmem_limit_bytes=58 << 20),
        name=body.__name__,
    )(*operands)


def down_scratch(level):
    ext = EXT[level]
    return [(ext + 2, ext + 16, LANES), (ext, ext, LANES), (ext // 2, ext, LANES), (2, 16, ext, LANES)]


def exchange(axis, to_next, to_previous):
    count = lax.axis_size(axis)
    onward = [(i, (i + 1) % count) for i in range(count)]
    backward = [((i + 1) % count, i) for i in range(count)]
    return lax.ppermute(to_next, axis, onward), lax.ppermute(to_previous, axis, backward)


def per_device(right_side, permittivity):
    both = (right_side, permittivity)
    xl, xr = exchange("gx", jnp.stack([b[24:] for b in both]), jnp.stack([b[:8] for b in both]))

    def y_slab(rows):
        middle = jnp.stack([b[:, rows] for b in both])
        return jnp.concatenate([xl[:, :, rows], middle, xr[:, :, rows]], axis=1)

    yl, yr = exchange("gy", y_slab(slice(24, 32)), y_slab(slice(0, 8)))
    p1, s0, v0 = kernel_call(
        down0, (shaped(16, 16, LANES),) + state_shapes(0), down_scratch(0),
        right_side, permittivity, xl, xr, yl, yr)

    xl, xr = exchange("gx", p1, p1)
    wide = jnp.concatenate([xl, p1, xr], axis=0)
    yl, yr = exchange("gy", wide, wide)
    p2, s1, v1 = kernel_call(
        down1, (shaped(16, 16, LANES),) + state_shapes(1), down_scratch(1), p1, xl, xr, yl, yr)

    xl, xr = exchange("gx", p2[:8], p2[8:])
    wide = jnp.concatenate([xl, p2, xr], axis=0)
    yl, yr = exchange("gy", wide[:, :8], wide[:, 8:])
    p3, s2, v2 = kernel_call(
        down2, (shaped(GX, 4, LANES),) + state_shapes(2), down_scratch(2) + [(2, 4, 8, LANES)],
        p2, xl, xr, yl, yr)

    column = lax.all_to_all(p3, "gx", 0, 0, tiled=True).reshape(4 * GX, LANES)
    gathered = lax.all_to_all(
        jnp.broadcast_to(column[None], (GY, 4 * GX, LANES)), "gy", 0, 0, tiled=True)

    rows = GY + 2
    scratch = [
        (2, rows, GX, LANES), (2, 7, GY, GX, LANES), (GY, GX, LANES), (2, rows, GX, LANES),
        (rows, GX, LANES), (GY, GX, LANES), (7, GY, GX, LANES), (rows, GX, LANES),
        (2, 16, 48, LANES), (2, 24, 64, LANES), (2, 24, 64, LANES), (12, 32, LANES), (17, 2, 48, LANES),
    ]
    return kernel_call(climb, shaped(32, 32, LANES), scratch, gathered, s0, v0, s1, v1, s2, v2)


def solution(mesh):
    placed = (P("gx", "gy", None), P("gx", "gy", None))
    return jax.shard_map(
        per_device, mesh=mesh, in_specs=placed, out_specs=P("gx", "gy", None), check_vma=False
    )
```

```python
import jax
import jax.numpy as jnp
from jax import lax
from jax.experimental import pallas as pl
from jax.experimental.pallas import tpu as pltpu
from jax.sharding import PartitionSpec as P

F32 = jnp.float32
LANES = 128
COARSE_SWEEPS = 12
OWN = (32, 16, 8)
HALO = (8, 16, 12)
EXT = (48, 48, 32)
GX = 8
GY = 32
CHUNK = 8


UNROLL = {"sweep": 6, "restrict": 4, "put": 16, "add": 4}
STOP = 99


def loop(first, last, body, step):
    def several(base, count):
        for store in [body(base + j) for j in range(count)]:
            store()

    whole = (last - first) // step
    if whole > 1:
        def one(i, carry):
            several(first + i * step, step)
            return carry

        lax.fori_loop(0, whole, one, 0)
    elif whole == 1:
        several(first, step)
    if (last - first) % step:
        several(first + whole * step, (last - first) % step)


def iota(shape, dim):
    return lax.broadcasted_iota(jnp.int32, shape, dim)


def lane_roll(v, shift):
    return pltpu.roll(v, shift % LANES, v.ndim - 1)


def flip(v, bit):
    lane = iota(v.shape, v.ndim - 1)
    return jnp.where((lane & bit) == 0, lane_roll(v, -bit), lane_roll(v, bit))


def pair_is_even(level, rows):
    shape = (rows, LANES)
    return ((iota(shape, 0) ^ (iota(shape, 1) >> level)) & 1) == 0


def bounds(level, index, count):
    own, halo, ext = OWN[level], HALO[level], EXT[level]
    low = halo - index * own
    high = halo + (count - index) * own
    return low, high


def clamp_edges(level, e, gx, gy):
    own, halo, ext = OWN[level], HALO[level], EXT[level]
    for back in range(-(-halo // own)):
        low = halo - back * own
        high = halo + own + back * own
        if low >= 1:

            @pl.when(gx == back)
            def _():
                e[low - 1] = e[low]

            @pl.when(gy == back)
            def _():
                e[:, 8 + low - 1 : 8 + low, :] = e[:, 8 + low : 8 + low + 1, :]

        if high < ext:

            @pl.when(gx == GX - 1 - back)
            def _():
                e[high] = e[high - 1]

            @pl.when(gy == GY - 1 - back)
            def _():
                e[:, 8 + high : 8 + high + 1, :] = e[:, 8 + high - 1 : 8 + high, :]


def prepare(level, first, last, e, f, state, total, v, gx, gy, after_pair=None):
    ext = EXT[level]
    step = 1 << level
    scale = 2.0 * 0.25**level

    def face(a, b):
        return scale * a * b / (a + b)

    xlow, xhigh = bounds(level, gx, GX)
    ylow, yhigh = bounds(level, gy, GY)
    shape = (8, LANES)
    lane = iota(shape, 1)
    z_last = (lane >> level) == (LANES >> level) - 1
    even = pair_is_even(level, 8)
    x_odd = jnp.where(even, 0, 1)

    def tile(p, r, before, below):
        mid = slice(8 + r, 16 + r)
        up = slice(9 + r, 17 + r)
        e0 = e[2 * p, mid, :]
        e1 = e[2 * p + 1, mid, :]
        after = e[2 * p + 2, mid, :]
        inner = face(e0, e1)
        outer0 = before
        outer1 = face(e1, after)
        yp0 = face(e0, e[2 * p, up, :])
        yp1 = face(e1, e[2 * p + 1, up, :])
        turned = pltpu.roll(yp0, 1, 0), pltpu.roll(yp1, 1, 0)
        if below is None:
            below = turned
        ym0, ym1 = (jnp.where(top, below[i], turned[i]) for i in range(2))
        zp0 = jnp.where(z_last, 0.0, face(e0, lane_roll(e0, -step)))
        zp1 = jnp.where(z_last, 0.0, face(e1, lane_roll(e1, -step)))
        zm0 = lane_roll(zp0, step)
        zm1 = lane_roll(zp1, step)
        f0 = f[2 * p, r : r + 8, :]
        f1 = f[2 * p + 1, r : r + 8, :]
        row = r + iota(shape, 0)
        y_ok = (row >= ylow) & (row < yhigh)
        for k in range(2):
            pick = even if k == 0 else jnp.logical_not(even)
            outer = jnp.where(pick, outer0, outer1)
            yp = jnp.where(pick, yp0, yp1)
            ym = jnp.where(pick, ym0, ym1)
            zp = jnp.where(pick, zp0, zp1)
            zm = jnp.where(pick, zm0, zm1)
            weight_sum = (inner + outer) + (yp + ym) + (zp + zm)
            x_at = 2 * p + (x_odd if k == 0 else 1 - x_odd)
            ok = y_ok & (x_at >= xlow) & (x_at < xhigh)
            inverse = jnp.where(ok, 1.0 / weight_sum, 0.0)
            source = jnp.where(pick, f0, f1) * inverse
            parts = (source, inner * inverse, outer * inverse, yp * inverse, ym * inverse,
                     zp * inverse, zm * inverse)
            for i in range(7):
                state[p, k, i, r : r + 8, :] = parts[i]
            if k == 0:
                total[p, r : r + 8, :] = weight_sum
                v[0, p, mid, :] = source
        return outer1, turned

    top = iota(shape, 0) == 0

    def body(p, carry):
        new, turned = [], None
        for c in range(ext // 8):
            outer, turned = tile(p, 8 * c, carry[c], turned)
            new.append(outer)
        if after_pair is not None:
            after_pair(p)
        return tuple(new)

    start = max(2 * first - 1, 0)
    init = tuple(face(e[start, 8 + 8 * c : 16 + 8 * c, :], e[2 * first, 8 + 8 * c : 16 + 8 * c, :])
                 for c in range(ext // 8))
    lax.fori_loop(first, last, body, init)


def clear(v, ext):
    def body(p, carry):
        for j in range(4):
            for k in range(2):
                v[k, 4 * p + j] = jnp.zeros((ext + 16, LANES), F32)
        return carry

    lax.fori_loop(0, ext // 8, body, 0)


def updated(level, k, p, v, state, low, high):
    step = 1 << level
    even = pair_is_even(level, high - low)
    mid = slice(8 + low, 8 + high)
    other = 1 - k
    here = v[other, p, mid, :]
    before = v[other, p - 1, mid, :]
    after = v[other, p + 1, mid, :]
    outer = jnp.where(even, before, after) if k == 0 else jnp.where(even, after, before)
    part = [state[p, k, 1 + i, low:high, :] for i in range(6)]
    x = part[0] * here + part[1] * outer
    y = part[2] * v[other, p, 9 + low : 9 + high, :] + part[3] * v[other, p, 7 + low : 7 + high, :]
    z = part[4] * lane_roll(here, -step) + part[5] * lane_roll(here, step)
    return (state[p, k, 0, low:high, :] + x) + (y + z)


def half_sweep(level, k, reach, v, state):
    own, halo, ext = OWN[level], HALO[level], EXT[level]
    first = (halo - reach) // 2
    last = (halo + own + reach + 1) // 2
    low = (halo - reach) // 8 * 8
    high = -(-(halo + own + reach) // 8) * 8

    def body(p):
        value = updated(level, k, p, v, state, low, high)

        def store():
            v[k, p, 8 + low : 8 + high, :] = value

        return store

    loop(first, last, body, UNROLL["sweep"])


def restrict(level, first, pairs, row, count, v, state, total, e, tmp, put):
    step = 1 << level
    low = row // 8 * 8
    high = -(-(row + 2 * count) // 8) * 8
    mid = slice(8 + low, 8 + high)

    def fine(q):
        p = first + q
        residual = (updated(level, 0, p, v, state, low, high) - v[0, p, mid, :]) * total[p, low:high, :]
        both = e[2 * p, mid, :] + e[2 * p + 1, mid, :]

        def store():
            tmp[0, q, low:high, :] = residual
            tmp[1, q, low:high, :] = both

        return store

    def coarse(q):
        out = []
        for i in range(2):
            a = tmp[i, q, pl.ds(row, count, stride=2), :] + tmp[i, q, pl.ds(row + 1, count, stride=2), :]
            out.append((a + flip(a, step)) * 0.125)
        return lambda: put(q, out[0], out[1])

    loop(0, pairs, fine, UNROLL["restrict"])
    loop(0, pairs, coarse, 2 * UNROLL["restrict"])


def interleave(f, e):
    return jnp.where((iota(f.shape, f.ndim - 1) & 1) == 0, f, e)


def split(both):
    low = (iota(both.shape, both.ndim - 1) & 1) == 0
    return jnp.where(low, both, lane_roll(both, 1)), jnp.where(low, lane_roll(both, -1), both)


def fill_rim(e, ext):
    e[ext : ext + 2] = jnp.ones((2, ext + 16, LANES), F32)
    e[0:ext, 0:8, :] = jnp.ones((ext, 8, LANES), F32)
    e[0:ext, 8 + ext :, :] = jnp.ones((ext, 8, LANES), F32)


def start_all(copies):
    for copy in copies:
        copy.start()


def wait_all(copies):
    for copy in copies:
        copy.wait()


KEPT = ((2, 22, 0, 48), (5, 19, 8, 40), (3, 13, 0, 32))
KEPT_V = ((1, 23), (4, 20), (2, 14))
GROUPS = 4


def state_copies(level, kept, vmem, sems):
    first, last, low, high = KEPT[level]
    copies = []
    for g in range(GROUPS):
        a = first + (last - first) * g // GROUPS
        b = first + (last - first) * (g + 1) // GROUPS
        copies.append((vmem.at[pl.ds(a, b - a), :, :, pl.ds(low, high - low), :],
                       kept.at[pl.ds(a - first, b - a)], sems.at[g], b - 1))
    return copies


def v_copy(level, kept_v, v, sem):
    first, last = KEPT_V[level]
    return v.at[:, pl.ds(first, last - first)], kept_v, sem


def sweep_down(level, pairs, reaches, inner, e, f, kept, kept_v, state, v, total, tmp, sems, gx, gy, put):
    clamp_edges(level, e, gx, gy)
    clear(v, EXT[level])
    outgoing = state_copies(level, kept, state, sems)

    def after_pair(p):
        for source, target, sem, last in outgoing:

            @pl.when(p == last)
            def _():
                pltpu.make_async_copy(source, target, sem).start()

    prepare(level, pairs[0], pairs[1], e, f, state, total, v, gx, gy, after_pair)
    if STOP >= 2:
        half_sweep(level, 1, reaches[0], v, state)
        half_sweep(level, 0, reaches[1], v, state)
        half_sweep(level, 1, reaches[2], v, state)
    source, target, sem = v_copy(level, kept_v, v, sems.at[GROUPS])
    v_out = pltpu.make_async_copy(source, target, sem)
    v_out.start()
    if STOP >= 3:
        restrict(level, *inner, v, state, total, e, tmp, put)
    for source, target, sem, last in outgoing:
        pltpu.make_async_copy(source, target, sem).wait()
    v_out.wait()


def down0(f_in, e_in, xl, xr, yl, yr, out, kept, kept_v, state, v, e, f, total, tmp, sems, in_sems):
    gx, gy = lax.axis_index("gx"), lax.axis_index("gy")
    copies = []
    for i, (target, own, off) in enumerate(((f, f_in, 0), (e, e_in, 8))):
        parts = (
            (xl.at[i], target.at[pl.ds(0, 8), pl.ds(off + 8, 32)]),
            (own, target.at[pl.ds(8, 32), pl.ds(off + 8, 32)]),
            (xr.at[i], target.at[pl.ds(40, 8), pl.ds(off + 8, 32)]),
            (yl.at[i], target.at[pl.ds(0, 48), pl.ds(off, 8)]),
            (yr.at[i], target.at[pl.ds(0, 48), pl.ds(off + 40, 8)]),
        )
        for j, (source, to) in enumerate(parts):
            copies.append(pltpu.make_async_copy(source, to, in_sems.at[5 * i + j]))
    start_all(copies)
    fill_rim(e, 48)
    wait_all(copies)

    def put(q, fc, ec):
        out[q] = interleave(fc, ec)

    if STOP >= 1:
        sweep_down(0, (0, 24), (6, 5, 4), (4, 16, 8, 16), e, f, kept, kept_v, state, v, total, tmp, sems, gx, gy, put)


def put_split(source, count, x, y, e, f):
    height = source.shape[1]

    def body(i):
        fi, ei = split(source[i])

        def store():
            f[x + i, y : y + height, :] = fi
            e[x + i, 8 + y : 8 + y + height, :] = ei

        return store

    loop(0, count, body, UNROLL["put"])


def down1(own, xl, xr, yl, yr, out, kept, kept_v, state, v, e, f, total, tmp, sems):
    gx, gy = lax.axis_index("gx"), lax.axis_index("gy")
    fill_rim(e, 48)
    put_split(xl, 16, 0, 16, e, f)
    put_split(own, 16, 16, 16, e, f)
    put_split(xr, 16, 32, 16, e, f)
    put_split(yl, 48, 0, 0, e, f)
    put_split(yr, 48, 0, 32, e, f)

    def put(q, fc, ec):
        out[q] = interleave(fc, ec)

    if STOP >= 1:
        sweep_down(1, (2, 22), (11, 10, 9), (4, 16, 8, 16), e, f, kept, kept_v, state, v, total, tmp, sems, gx, gy, put)


def down2(own, xl, xr, yl, yr, out, kept, kept_v, state, v, e, f, total, tmp, sems, coarse):
    gx, gy = lax.axis_index("gx"), lax.axis_index("gy")
    fill_rim(e, 32)
    put_split(xl, 8, 0, 8, e, f)
    put_split(own, 16, 8, 8, e, f)
    put_split(xr, 8, 24, 8, e, f)
    put_split(yl, 32, 0, 0, e, f)
    put_split(yr, 32, 0, 24, e, f)

    def put(q, fc, ec):
        coarse[0, q, 0:4, :] = fc
        coarse[1, q, 0:4, :] = ec

    if STOP >= 1:
        sweep_down(2, (1, 15), (9, 8, 7), (6, 4, 12, 4), e, f, kept, kept_v, state, v, total, tmp, sems, gx, gy, put)
    slot = iota((1, LANES), 1) & 7
    for i in range(2):
        for r in range(2):
            row = jnp.zeros((1, LANES), F32)
            for x1 in range(2):
                for y in range(4):
                    row = jnp.where(slot == 4 * x1 + y, coarse[i, 2 * x1 + r, y : y + 1, :], row)
            out[:, 2 * i + r : 2 * i + r + 1, :] = jnp.broadcast_to(row[None], (GX, 1, LANES))


BLOCK = (CHUNK, GX, LANES)


def pair_before(v, fill):
    axis = v.ndim - 2
    low = (iota(v.shape, v.ndim - 1) & 4) == 0
    moved = jnp.where(low, pltpu.roll(lane_roll(v, -4), 1, axis), lane_roll(v, 4))
    return jnp.where(low & (iota(v.shape, axis) == 0), fill, moved)


def pair_after(v, fill):
    axis = v.ndim - 2
    high = (iota(v.shape, v.ndim - 1) & 4) != 0
    moved = jnp.where(high, pltpu.roll(lane_roll(v, 4), GX - 1, axis), lane_roll(v, -4))
    return jnp.where(high & (iota(v.shape, axis) == GX - 1), fill, moved)


def y_after(level, v, following):
    lane = iota(v.shape, v.ndim - 1)
    if level == 3:
        return jnp.where((lane & 3) == 3, lane_roll(following, 3), lane_roll(v, -1))
    return jnp.where((lane & 2) == 2, lane_roll(following, 2), lane_roll(v, -2))


def y_before(level, v, preceding):
    lane = iota(v.shape, v.ndim - 1)
    if level == 3:
        return jnp.where((lane & 3) == 0, lane_roll(preceding, -3), lane_roll(v, 1))
    return jnp.where((lane & 2) == 0, lane_roll(preceding, -2), lane_roll(v, 2))


def slots(shape):
    lane = iota(shape, len(shape) - 1)
    return (lane & 1) | ((lane >> 2) & 2)


def tiles_from_slots(parts):
    slot = slots(parts[0].shape)
    return jnp.where(slot == 0, parts[0], jnp.where(slot == 1, parts[1], jnp.where(slot == 2, parts[2], parts[3])))


def slot_after(v, fill):
    slot = slots(v.shape)
    return jnp.where(slot == 3, fill, jnp.where(slot == 1, lane_roll(v, -7), lane_roll(v, -1)))


def slot_before(v, fill):
    slot = slots(v.shape)
    return jnp.where(slot == 0, fill, jnp.where(slot == 2, lane_roll(v, 7), lane_roll(v, 1)))


def coarse_levels(f3, e3, s3, w3, v3, s4):
    lane = iota(BLOCK, 2)
    even3 = ((lane ^ (lane >> 3)) & 1) == 0
    z_last3 = (lane >> 3) == 15
    chunks = range(0, GY, CHUNK)

    def face(scale, a, b):
        return (2.0 * scale) * a * b / (a + b)

    zero = jnp.zeros((GX, LANES), F32)
    for k in range(2):
        e3[k, 0] = lane_roll(e3[k, 1], 3)
        e3[k, 1 + GY] = lane_roll(e3[k, GY], -3)
        v3[k, 0] = zero
        v3[k, 1 + GY] = zero
    scale = 0.25**3
    e4 = []
    for g in chunks:
        here = pl.ds(1 + g, CHUNK)
        both = (e3[0, here], e3[1, here])
        inner = face(scale, both[0], both[1])
        outer = (face(scale, both[0], pair_before(both[1], both[0])),
                 face(scale, both[1], pair_after(both[0], both[1])))
        yp, ym, zp, zm, f = [], [], [], [], []
        for r in range(2):
            own = both[r]
            yp.append(face(scale, own, y_after(3, own, e3[r, pl.ds(2 + g, CHUNK)])))
            ym.append(face(scale, own, y_before(3, own, e3[r, pl.ds(g, CHUNK)])))
            z = jnp.where(z_last3, 0.0, face(scale, own, lane_roll(own, -8)))
            zp.append(z)
            zm.append(lane_roll(z, 8))
            f.append(f3[r, pl.ds(g, CHUNK)])
        for k in range(2):
            a, b = k, 1 - k
            parts = [jnp.where(even3, t[a], t[b]) for t in (outer, yp, ym, zp, zm)]
            weight_sum = inner
            for t in parts:
                weight_sum = weight_sum + t
            inverse = 1.0 / weight_sum
            source = jnp.where(even3, f[a], f[b]) * inverse
            s3[k, 0, pl.ds(g, CHUNK)] = source
            s3[k, 1, pl.ds(g, CHUNK)] = inner * inverse
            for i in range(5):
                s3[k, 2 + i, pl.ds(g, CHUNK)] = parts[i] * inverse
            if k == 0:
                w3[pl.ds(g, CHUNK)] = weight_sum
                v3[0, here] = source
        t = both[0] + both[1]
        t = t + flip(t, 1)
        e4.append((t + flip(t, 8)) * 0.125)

    def update3(k, g):
        o = 1 - k
        own = v3[o, pl.ds(1 + g, CHUNK)]
        before, after = pair_before(own, 0.0), pair_after(own, 0.0)
        outer = jnp.where(even3, before, after) if k == 0 else jnp.where(even3, after, before)
        sides = (own, outer, y_after(3, own, v3[o, pl.ds(2 + g, CHUNK)]),
                 y_before(3, own, v3[o, pl.ds(g, CHUNK)]), lane_roll(own, -8), lane_roll(own, 8))
        part = [s3[k, 1 + i, pl.ds(g, CHUNK)] * sides[i] for i in range(6)]
        return ((s3[k, 0, pl.ds(g, CHUNK)] + part[0]) + (part[1] + part[2])) + ((part[3] + part[4]) + part[5])

    def sweep3(k):
        for g in chunks:
            v3[k, pl.ds(1 + g, CHUNK)] = update3(k, g)

    sweep3(1)
    sweep3(0)
    sweep3(1)
    f4 = []
    for g in chunks:
        t = (update3(0, g) - v3[0, pl.ds(1 + g, CHUNK)]) * w3[pl.ds(g, CHUNK)]
        t = t + flip(t, 1)
        f4.append((t + flip(t, 8)) * 0.125)

    e4 = tiles_from_slots(e4)
    f4 = tiles_from_slots(f4)
    e4 = [e4[b] for b in range(CHUNK)]
    tile = (GX, LANES)
    lane = iota(tile, 1)
    even4 = (((lane >> 1) ^ (lane >> 2) ^ (lane >> 4)) & 1) == 0
    z_last4 = (lane >> 4) == 7
    scale = 0.25**4
    e_after = e4[1:] + [slot_after(e4[0], lane_roll(e4[-1], -2))]
    e_before = [slot_before(e4[-1], lane_roll(e4[0], 2))] + e4[:-1]
    v = []
    for b in range(CHUNK):
        own = e4[b]
        z = jnp.where(z_last4, 0.0, face(scale, own, lane_roll(own, -16)))
        parts = [face(scale, own, pair_before(own, own)), face(scale, own, pair_after(own, own)),
                 face(scale, own, y_after(4, own, e_after[b])), face(scale, own, y_before(4, own, e_before[b])),
                 z, lane_roll(z, 16)]
        weight_sum = parts[0]
        for t in parts[1:]:
            weight_sum = weight_sum + t
        inverse = 1.0 / weight_sum
        source = f4[b] * inverse
        s4[0, b] = source
        for i in range(6):
            s4[1 + i, b] = parts[i] * inverse
        v.append(jnp.where(even4, source, 0.0))

    def sweep4(k, v):
        v = list(v)
        after = v[1:] + [slot_after(v[0], 0.0)]
        before = [slot_before(v[-1], 0.0)] + v[:-1]
        new = []
        for b in range(CHUNK):
            own = v[b]
            x = s4[1, b] * pair_before(own, 0.0) + s4[2, b] * pair_after(own, 0.0)
            y = s4[3, b] * y_after(4, own, after[b]) + s4[4, b] * y_before(4, own, before[b])
            z = s4[5, b] * lane_roll(own, -16) + s4[6, b] * lane_roll(own, 16)
            value = (s4[0, b] + z) + (x + y)
            new.append(jnp.where(even4, value, own) if k == 0 else jnp.where(even4, own, value))
        return tuple(new)

    v = sweep4(1, v)
    if STOP >= 11:
        v = lax.fori_loop(0, COARSE_SWEEPS - 1, lambda i, v: sweep4(1, sweep4(0, v)), v)
    v = jnp.stack(v)
    slot = slots(BLOCK)
    for a, g in enumerate(chunks):
        here = pl.ds(1 + g, CHUNK)
        u = jnp.where(slot == a, v, 0.0)
        u = u + flip(u, 1)
        u = u + flip(u, 8)
        v3[0, here] = v3[0, here] + u
        v3[1, here] = v3[1, here] + u
    if STOP < 12:
        return
    sweep3(0)
    sweep3(1)
    sweep3(0)
    sweep3(1)


def around_from_level3(v3, up, gx, gy):
    shape = (GX, LANES)
    lane, sub = iota(shape, 1), iota(shape, 0)
    even3 = ((lane ^ (lane >> 3)) & 1) == 0
    head = (lane & 7) == 0
    outside = ((sub == 0) & (gx == 0)) | ((sub == 2) & (gx == GX - 1))
    up[...] = jnp.zeros(up.shape, F32)
    for dy in range(3):
        red = v3[0, gy + dy]
        black = v3[1, gy + dy]
        for r in range(2):
            t = jnp.where(even3, red, black) if r == 0 else jnp.where(even3, black, red)
            t = jnp.where(outside, 0.0, pltpu.roll(t, lax.rem(GX + 1 - gx, GX), 0))
            for s in range(8):
                w = jnp.where(head, lane_roll(t, -s), 0.0)
                w = w + lane_roll(w, 1)
                w = w + lane_roll(w, 2)
                w = w + lane_roll(w, 4)
                for dx in range(3):
                    x = 4 * dx + 2 * (s // 4) + r
                    y = 4 + 2 * (4 * dy + s % 4)
                    up[x, y : y + 2, :] = jnp.broadcast_to(w[dx : dx + 1], (2, LANES))


def climb(near, far, k0, kv0, k1, kv1, k2, kv2, out, f3, e3, s3, w3, v3, s4, v2, v1, v0,
          up3, up, s0, s1, s2, i0, i1, i2, sems, v_sems):
    gx, gy = lax.axis_index("gx"), lax.axis_index("gy")
    loads = []
    for level, kept, kept_v, state, v_in in ((2, k2, kv2, s2, i2), (1, k1, kv1, s1, i1), (0, k0, kv0, s0, i0)):
        first, last, low, high = KEPT[level]
        loads.append((
            pltpu.make_async_copy(kept, state.at[pl.ds(first, last - first), :, :, pl.ds(low, high - low), :],
                                  sems.at[level]),
            pltpu.make_async_copy(kept_v, v_in, v_sems.at[level]),
        ))
    for pair in loads:
        start_all(pair)
    clear(v2, 32)
    clear(v1, 48)
    clear(v0, 48)
    for c, held in enumerate((near, far)):
        for dx in range(4):
            for dy in range(4):
                g = (((gy // 8 + dx) & 3) * 4 + ((gy // 2 + dy) & 3)) * 2 + (gy & 1 if c == 0 else 1 - (gy & 1))
                for r in range(2):
                    f3[r, g] = held[dx, dy, pl.ds(r, GX, stride=4), :]
                    e3[r, 1 + g] = held[dx, dy, pl.ds(2 + r, GX, stride=4), :]
    coarse_levels(f3, e3, s3, w3, v3, s4)
    around_from_level3(v3, up3, gx, gy)

    wait_all(loads[0])
    if STOP >= 13:

        def add2(p):
            new = [i2[k, p - KEPT_V[2][0], 8:40, :] + up3[p - 2] for k in range(2)]

            def store():
                for k in range(2):
                    v2[k, p, 8:40, :] = new[k]

            return store

        loop(2, 14, add2, UNROLL["add"])
        half_sweep(2, 0, 6, v2, s2)
        half_sweep(2, 1, 5, v2, s2)
        half_sweep(2, 0, 4, v2, s2)
        half_sweep(2, 1, 3, v2, s2)

    def raised(level, first, last, offset, coarse_v, v_in, v):
        base = KEPT_V[level][0]

        def doubled(c):
            rows = 24
            even = pair_is_even(level + 1, rows)
            start = 8 + (12 if level == 0 else 4)
            red = coarse_v[0, c, start : start + rows, :]
            black = coarse_v[1, c, start : start + rows, :]
            both = (jnp.where(even, red, black), jnp.where(even, black, red))

            def store():
                for s in range(2):
                    for twice in range(2):
                        up[c, s, pl.ds(twice, rows, stride=2), :] = both[s]

            return store

        loop(first, last, doubled, 2)

        def add(c):
            new = [(k, 2 * c - offset + s, v_in[k, 2 * c - offset + s - base, 8:56, :] + up[c, s])
                   for s in range(2) for k in range(2)]

            def store():
                for k, p, value in new:
                    v[k, p, 8:56, :] = value

            return store

        loop(first, last, add, 1)

    wait_all(loads[1])
    if STOP >= 14:
        raised(1, 4, 12, 4, v2, i1, v1)
        half_sweep(1, 0, 5, v1, s1)
        half_sweep(1, 1, 4, v1, s1)
        half_sweep(1, 0, 3, v1, s1)
        half_sweep(1, 1, 2, v1, s1)

    wait_all(loads[2])
    if STOP >= 15:
        raised(0, 7, 17, 12, v1, i0, v0)
        half_sweep(0, 0, 3, v0, s0)
        half_sweep(0, 1, 2, v0, s0)
        half_sweep(0, 0, 1, v0, s0)
        half_sweep(0, 1, 0, v0, s0)
    even = pair_is_even(0, 32)

    def finish(q):
        red = v0[0, 4 + q, 16:48, :]
        black = v0[1, 4 + q, 16:48, :]

        def store():
            out[2 * q] = jnp.where(even, red, black)
            out[2 * q + 1] = jnp.where(even, black, red)

        return store

    loop(0, 16, finish, 4)


def shaped(*dims):
    return jax.ShapeDtypeStruct(dims, F32)


def kept_shapes(level):
    first, last, low, high = KEPT[level]
    v_first, v_last = KEPT_V[level]
    return (shaped(last - first, 2, 7, high - low, LANES),
            shaped(2, v_last - v_first, EXT[level] + 16, LANES))


def down_scratch(level):
    ext = EXT[level]
    vmem = [(ext // 2, 2, 7, ext, LANES), (2, ext // 2, ext + 16, LANES), (ext + 2, ext + 16, LANES),
            (ext, ext, LANES), (ext // 2, ext, LANES), (2, 16, ext, LANES)]
    return [pltpu.VMEM(s, F32) for s in vmem] + [pltpu.SemaphoreType.DMA((GROUPS + 1,))]


def kernel_call(body, in_spaces, out_shape, out_spaces, scratch, mib, *operands):
    def specs(spaces):
        return [pl.BlockSpec(memory_space=pltpu.VMEM if s == "v" else pl.ANY) for s in spaces]

    return pl.pallas_call(
        body,
        in_specs=specs(in_spaces),
        out_specs=tuple(specs(out_spaces)),
        out_shape=tuple(out_shape),
        scratch_shapes=scratch,
        compiler_params=pltpu.CompilerParams(vmem_limit_bytes=mib << 20),
        name=body.__name__,
    )(*operands)


def exchange(axis, to_next, to_previous):
    count = lax.axis_size(axis)
    onward = [(i, (i + 1) % count) for i in range(count)]
    backward = [((i + 1) % count, i) for i in range(count)]
    return lax.ppermute(to_next, axis, onward), lax.ppermute(to_previous, axis, backward)


def from_offset(values, dx, dy, dc):
    moves = []
    for g in range(GY):
        x, y, c = g // 8, (g // 2) % 4, g % 2
        moves.append((((x + dx) % 4 * 4 + (y + dy) % 4) * 2 + (c ^ dc), g))
    return lax.ppermute(values, "gy", moves)


def per_device(right_side, permittivity):
    both = (right_side, permittivity)
    xl, xr = exchange("gx", jnp.stack([b[24:] for b in both]), jnp.stack([b[:8] for b in both]))

    def y_slab(rows):
        middle = jnp.stack([b[:, rows] for b in both])
        return jnp.concatenate([xl[:, :, rows], middle, xr[:, :, rows]], axis=1)

    yl, yr = exchange("gy", y_slab(slice(24, 32)), y_slab(slice(0, 8)))
    p1, s0, v0 = kernel_call(
        down0, "aavvvv", (shaped(16, 16, LANES),) + kept_shapes(0), "vaa",
        down_scratch(0) + [pltpu.SemaphoreType.DMA((10,))], 24,
        right_side, permittivity, xl, xr, yl, yr)

    xl, xr = exchange("gx", p1, p1)
    wide = jnp.concatenate([xl, p1, xr], axis=0)
    yl, yr = exchange("gy", wide, wide)
    p2, s1, v1 = kernel_call(
        down1, "vvvvv", (shaped(16, 16, LANES),) + kept_shapes(1), "vaa", down_scratch(1), 24, p1, xl, xr, yl, yr)

    xl, xr = exchange("gx", p2[:8], p2[8:])
    wide = jnp.concatenate([xl, p2, xr], axis=0)
    yl, yr = exchange("gy", wide[:, :8], wide[:, 8:])
    p3, s2, v2 = kernel_call(
        down2, "vvvvv", (shaped(GX, 4, LANES),) + kept_shapes(2), "vaa",
        down_scratch(2) + [pltpu.VMEM((2, 4, 8, LANES), F32)], 14, p2, xl, xr, yl, yr)

    column = lax.all_to_all(p3, "gx", 0, 0, tiled=True).reshape(4 * GX, LANES)
    along_y = jnp.stack([column] + [from_offset(column, 0, d, 0) for d in (1, 2, 3)])
    near = jnp.stack([along_y] + [from_offset(along_y, d, 0, 0) for d in (1, 2, 3)])
    far = from_offset(near, 0, 0, 1)
    return climb_call(near, far, s0, v0, s1, v1, s2, v2)


def climb_call(*operands):
    rows = GY + 2
    vmem = [
        (2, GY, GX, LANES), (2, rows, GX, LANES), (2, 7, GY, GX, LANES), (GY, GX, LANES), (2, rows, GX, LANES),
        (7, CHUNK, GX, LANES),
        (2, 16, 48, LANES), (2, 24, 64, LANES), (2, 24, 64, LANES), (12, 32, LANES), (17, 2, 48, LANES),
    ]
    vmem += [(EXT[l] // 2, 2, 7, EXT[l], LANES) for l in range(3)]
    vmem += [kept_shapes(l)[1].shape for l in range(3)]
    scratch = [pltpu.VMEM(s, F32) for s in vmem] + [pltpu.SemaphoreType.DMA((3,))] * 2
    return kernel_call(climb, "vvaaaaaa", (shaped(32, 32, LANES),), "v", scratch, 36, *operands)[0]


def solution(mesh):
    placed = (P("gx", "gy", None), P("gx", "gy", None))
    return jax.shard_map(
        per_device, mesh=mesh, in_specs=placed, out_specs=P("gx", "gy", None), check_vma=False
    )
```

```python
import jax
import jax.numpy as jnp
from jax import lax
from jax.experimental import pallas as pl
from jax.experimental.pallas import tpu as pltpu
from jax.sharding import PartitionSpec as P

F32 = jnp.float32
LANES = 128
COARSE_SWEEPS = 12
OWN = (32, 16, 8)
HALO = (8, 16, 12)
EXT = (48, 48, 32)
GX = 8
GY = 32
CHUNK = 8
C3 = 1
KEPT = (5, 19, 8, 40)
GROUPS = 4


UNROLL = {"sweep": 6, "restrict": 4, "put": 16, "add": 4}
STOP = 99
KEPT_SPEC = "vvv"


def loop(first, last, body, step):
    def several(base, count):
        for store in [body(base + j) for j in range(count)]:
            store()

    whole = (last - first) // step
    if whole > 1:
        def one(i, carry):
            several(first + i * step, step)
            return carry

        lax.fori_loop(0, whole, one, 0)
    elif whole == 1:
        several(first, step)
    if (last - first) % step:
        several(first + whole * step, (last - first) % step)


def iota(shape, dim):
    return lax.broadcasted_iota(jnp.int32, shape, dim)


def lane_roll(v, shift):
    return pltpu.roll(v, shift % LANES, v.ndim - 1)


def flip(v, bit):
    lane = iota(v.shape, v.ndim - 1)
    return jnp.where((lane & bit) == 0, lane_roll(v, -bit), lane_roll(v, bit))


def pair_is_even(level, rows):
    shape = (rows, LANES)
    return ((iota(shape, 0) ^ (iota(shape, 1) >> level)) & 1) == 0


def bounds(level, index, count):
    own, halo, ext = OWN[level], HALO[level], EXT[level]
    low = halo - index * own
    high = halo + (count - index) * own
    return low, high


def clamp_edges(level, e, gx, gy):
    own, halo, ext = OWN[level], HALO[level], EXT[level]
    for back in range(-(-halo // own)):
        low = halo - back * own
        high = halo + own + back * own
        if low >= 1:

            @pl.when(gx == back)
            def _():
                e[low - 1] = e[low]

            @pl.when(gy == back)
            def _():
                e[0:ext, 8 + low - 1 : 8 + low, :] = e[0:ext, 8 + low : 8 + low + 1, :]

        if high < ext:

            @pl.when(gx == GX - 1 - back)
            def _():
                e[high] = e[high - 1]

            @pl.when(gy == GY - 1 - back)
            def _():
                e[0:ext, 8 + high : 8 + high + 1, :] = e[0:ext, 8 + high - 1 : 8 + high, :]


def faces(pairs):
    sums = [a + b for a, b in pairs]
    first = sums[0] * sums[1]
    whole = 1.0 / (first * sums[2])
    rest = whole * sums[2]
    inverse = (rest * sums[1], rest * sums[0], whole * first)
    return [a * b * i for (a, b), i in zip(pairs, inverse)]


def inverses(a, b):
    whole = 1.0 / (a * b)
    return whole * b, whole * a


def prepare(level, first, last, e, f, state, total, v, gx, gy, after_pair=None):
    ext = EXT[level]
    step = 1 << level
    source_scale = 0.5 * 4.0**level

    xlow, xhigh = bounds(level, gx, GX)
    ylow, yhigh = bounds(level, gy, GY)
    shape = (8, LANES)
    lane = iota(shape, 1)
    z_last = (lane >> level) == (LANES >> level) - 1
    even = pair_is_even(level, 8)
    aligned = all((HALO[level] + i * OWN[level]) % 8 == 0 for i in range(2))

    def tile(p, r, before, below):
        mid = slice(8 + r, 16 + r)
        up = slice(9 + r, 17 + r)
        e0 = e[2 * p, mid, :]
        e1 = e[2 * p + 1, mid, :]
        after = e[2 * p + 2, mid, :]
        outer0 = before
        inner, outer1, yp0 = faces(((e0, e1), (e1, after), (e0, e[2 * p, up, :])))
        yp1, zp0, zp1 = faces(((e1, e[2 * p + 1, up, :]), (e0, lane_roll(e0, -step)), (e1, lane_roll(e1, -step))))
        zp0 = jnp.where(z_last, 0.0, zp0)
        zp1 = jnp.where(z_last, 0.0, zp1)
        turned = pltpu.roll(yp0, 1, 0), pltpu.roll(yp1, 1, 0)
        if below is None:
            below = turned
        ym0, ym1 = (jnp.where(top, below[i], turned[i]) for i in range(2))
        zm0 = lane_roll(zp0, step)
        zm1 = lane_roll(zp1, step)
        f0 = f[2 * p, r : r + 8, :]
        f1 = f[2 * p + 1, r : r + 8, :]
        ok = (2 * p >= xlow) & (2 * p < xhigh)
        if aligned:
            ok = jnp.where(ok & (r >= ylow) & (r < yhigh), 1.0, 0.0)
        else:
            row = r + iota(shape, 0)
            ok = jnp.where(ok, 1.0, 0.0) * jnp.where((row >= ylow) & (row < yhigh), 1.0, 0.0)
        sides, sums = [], []
        for k in range(2):
            pick = even if k == 0 else jnp.logical_not(even)
            side = [inner] + [jnp.where(pick, a, b) for a, b in (
                (outer0, outer1), (yp0, yp1), (ym0, ym1), (zp0, zp1), (zm0, zm1))]
            sides.append(side)
            sums.append((side[0] + side[1]) + (side[2] + side[3]) + (side[4] + side[5]))
        inverse = inverses(*sums)
        for k in range(2):
            scaled = inverse[k] * ok
            source = (jnp.where(even, f0, f1) if k == 0 else jnp.where(even, f1, f0)) * (scaled * source_scale)
            state[p, k, 0, r : r + 8, :] = source
            for i in range(6):
                state[p, k, 1 + i, r : r + 8, :] = sides[k][i] * scaled
            if k == 0:
                total[p, r : r + 8, :] = sums[0]
                v[0, p, mid, :] = source
        return outer1, turned

    top = iota(shape, 0) == 0

    def body(p, carry):
        new, turned = [], None
        for c in range(ext // 8):
            outer, turned = tile(p, 8 * c, carry[c], turned)
            new.append(outer)
        if after_pair is not None:
            after_pair(p)
        return tuple(new)

    start = max(2 * first - 1, 0)
    init = []
    for c in range(ext // 8):
        a, b = e[start, 8 + 8 * c : 16 + 8 * c, :], e[2 * first, 8 + 8 * c : 16 + 8 * c, :]
        init.append(a * b / (a + b))
    init = tuple(init)
    lax.fori_loop(first, last, body, init)


def clear(v, ext):
    def body(p, carry):
        for j in range(4):
            for k in range(2):
                v[k, 4 * p + j] = jnp.zeros((ext + 16, LANES), F32)
        return carry

    lax.fori_loop(0, ext // 8, body, 0)


def updated(level, k, p, v, state, low, high, base=(0, 0)):
    step = 1 << level
    even = pair_is_even(level, high - low)
    mid = slice(8 + low, 8 + high)
    other = 1 - k
    here = v[other, p, mid, :]
    before = v[other, p - 1, mid, :]
    after = v[other, p + 1, mid, :]
    outer = jnp.where(even, before, after) if k == 0 else jnp.where(even, after, before)
    rows = slice(low - base[1], high - base[1])
    part = [state[p - base[0], k, 1 + i, rows, :] for i in range(6)]
    x = part[0] * here + part[1] * outer
    y = part[2] * v[other, p, 9 + low : 9 + high, :] + part[3] * v[other, p, 7 + low : 7 + high, :]
    z = part[4] * lane_roll(here, -step) + part[5] * lane_roll(here, step)
    return (state[p - base[0], k, 0, rows, :] + x) + (y + z)


def half_sweep(level, k, reach, v, state, base=(0, 0)):
    own, halo, ext = OWN[level], HALO[level], EXT[level]
    first = (halo - reach) // 2
    last = (halo + own + reach + 1) // 2
    low = (halo - reach) // 8 * 8
    high = -(-(halo + own + reach) // 8) * 8

    def body(p):
        value = updated(level, k, p, v, state, low, high, base)

        def store():
            v[k, p, 8 + low : 8 + high, :] = value

        return store

    loop(first, last, body, UNROLL["sweep"])


def restrict(level, first, pairs, row, count, v, state, total, e, tmp, put):
    step = 1 << level
    low = row // 8 * 8
    high = -(-(row + 2 * count) // 8) * 8
    mid = slice(8 + low, 8 + high)

    def fine(q):
        p = first + q
        residual = (updated(level, 0, p, v, state, low, high) - v[0, p, mid, :]) * total[p, low:high, :]
        both = e[2 * p, mid, :] + e[2 * p + 1, mid, :]

        def store():
            tmp[0, q, low:high, :] = residual
            tmp[1, q, low:high, :] = both

        return store

    def coarse(q):
        out = []
        for i in range(2):
            a = tmp[i, q, pl.ds(row, count, stride=2), :] + tmp[i, q, pl.ds(row + 1, count, stride=2), :]
            out.append((a + flip(a, step)) * (0.125 if i else 0.25 * 0.25**level))
        return lambda: put(q, out[0], out[1])

    loop(0, pairs, fine, UNROLL["restrict"])
    loop(0, pairs, coarse, 2 * UNROLL["restrict"])


def interleave(f, e):
    return jnp.where((iota(f.shape, f.ndim - 1) & 1) == 0, f, e)


def split(both):
    low = (iota(both.shape, both.ndim - 1) & 1) == 0
    return jnp.where(low, both, lane_roll(both, 1)), jnp.where(low, lane_roll(both, -1), both)


def fill_rim(e, ext):
    e[ext : ext + 2] = jnp.ones((2, ext + 16, LANES), F32)
    e[0:ext, 0:8, :] = jnp.ones((ext, 8, LANES), F32)
    e[0:ext, 8 + ext :, :] = jnp.ones((ext, 8, LANES), F32)


def start_all(copies):
    for copy in copies:
        copy.start()


def wait_all(copies):
    for copy in copies:
        copy.wait()


def sweep_down(level, pairs, reaches, inner, e, f, state, v, total, tmp, gx, gy, put, after_pair=None):
    clamp_edges(level, e, gx, gy)
    prepare(level, pairs[0], pairs[1], e, f, state, total, v, gx, gy, after_pair)
    if STOP >= 2:
        half_sweep(level, 1, reaches[0], v, state)
        half_sweep(level, 0, reaches[1], v, state)
        half_sweep(level, 1, reaches[2], v, state)
    if STOP >= 3:
        restrict(level, *inner, v, state, total, e, tmp, put)


def down0(f_in, e_in, xl, xr, yl, yr, cl, cr, out, state, v, e, f, total, tmp, in_sems):
    gx, gy = lax.axis_index("gx"), lax.axis_index("gy")
    ya, yb = 0, 40
    copies = []
    for i, (target, own, off) in enumerate(((f, f_in, 0), (e, e_in, 8))):
        parts = (
            (xl.at[i], target.at[pl.ds(0, 8), pl.ds(off + 8, 32)]),
            (own, target.at[pl.ds(8, 32), pl.ds(off + 8, 32)]),
            (xr.at[i], target.at[pl.ds(40, 8), pl.ds(off + 8, 32)]),
            (yl.at[i], target.at[pl.ds(8, 32), pl.ds(off + ya, 8)]),
            (yr.at[i], target.at[pl.ds(8, 32), pl.ds(off + yb, 8)]),
            (cl.at[i, pl.ds(0, 8)], target.at[pl.ds(0, 8), pl.ds(off + ya, 8)]),
            (cl.at[i, pl.ds(8, 8)], target.at[pl.ds(40, 8), pl.ds(off + ya, 8)]),
            (cr.at[i, pl.ds(0, 8)], target.at[pl.ds(0, 8), pl.ds(off + yb, 8)]),
            (cr.at[i, pl.ds(8, 8)], target.at[pl.ds(40, 8), pl.ds(off + yb, 8)]),
        )
        for j, (source, to) in enumerate(parts):
            copies.append(pltpu.make_async_copy(source, to, in_sems.at[9 * i + j]))
    start_all(copies)
    fill_rim(e, 48)
    clear(v, 48)
    wait_all(copies)

    def put(q, fc, ec):
        out[q] = interleave(fc, ec)

    if STOP >= 1:
        sweep_down(0, (0, 24), (6, 5, 4), (4, 16, 8, 16), e, f, state, v, total, tmp, gx, gy, put)


def put_split(source, start, count, x, y, e, f):
    height = source.shape[1]

    def body(i):
        fi, ei = split(source[start + i])

        def store():
            f[x + i, pl.ds(y, height), :] = fi
            e[x + i, pl.ds(8 + y, height), :] = ei

        return store

    loop(0, count, body, UNROLL["put"])


def down1(own, xl, xr, yl, yr, cl, cr, out, kept, v, e, f, total, tmp, state, sems):
    gx, gy = lax.axis_index("gx"), lax.axis_index("gy")
    fill_rim(e, 48)
    clear(v, 48)
    put_split(xl, 0, 13, 3, 16, e, f)
    put_split(own, 0, 16, 16, 16, e, f)
    put_split(xr, 0, 13, 32, 16, e, f)
    for side, corner, y in ((yl, cl, 0), (yr, cr, 32)):
        put_split(corner, 0, 13, 3, y, e, f)
        put_split(side, 0, 16, 16, y, e, f)
        put_split(corner, 13, 13, 32, y, e, f)

    def put(q, fc, ec):
        out[q] = interleave(fc, ec)

    first, last, low, high = KEPT
    copies = []
    for g in range(GROUPS):
        a = first + (last - first) * g // GROUPS
        b = first + (last - first) * (g + 1) // GROUPS
        copies.append((b - 1, pltpu.make_async_copy(
            state.at[pl.ds(a, b - a), :, :, pl.ds(low, high - low), :], kept.at[pl.ds(a - first, b - a)], sems.at[g])))

    def after_pair(p):
        for end, copy in copies:

            @pl.when(p == end)
            def _():
                copy.start()

    sweep_down(1, (2, 22), (11, 10, 9), (4, 16, 8, 16), e, f, state, v, total, tmp, gx, gy, put, after_pair)
    wait_all([copy for _, copy in copies])


def down2(own, xl, xr, yl, yr, cl, cr, out, state, v, e, f, total, tmp, coarse):
    gx, gy = lax.axis_index("gx"), lax.axis_index("gy")
    fill_rim(e, 32)
    clear(v, 32)
    put_split(xl, 0, 8, 0, 8, e, f)
    put_split(own, 0, 16, 8, 8, e, f)
    put_split(xr, 0, 8, 24, 8, e, f)
    for side, corner, y in ((yl, cl, 0), (yr, cr, 24)):
        put_split(corner, 0, 8, 0, y, e, f)
        put_split(side, 0, 16, 8, y, e, f)
        put_split(corner, 8, 8, 24, y, e, f)

    def put(q, fc, ec):
        coarse[0, q, 0:4, :] = fc
        coarse[1, q, 0:4, :] = ec

    if STOP >= 1:
        sweep_down(2, (1, 15), (9, 8, 7), (6, 4, 12, 4), e, f, state, v, total, tmp, gx, gy, put)
    slot = iota((1, LANES), 1) & 7
    for i in range(2):
        for r in range(2):
            row = jnp.zeros((1, LANES), F32)
            for x1 in range(2):
                for y in range(4):
                    row = jnp.where(slot == 4 * x1 + y, coarse[i, 2 * x1 + r, y : y + 1, :], row)
            out[:, 2 * i + r : 2 * i + r + 1, :] = jnp.broadcast_to(row[None], (GX, 1, LANES))


BLOCK = (CHUNK, GX, LANES)


def pair_before(v, fill):
    axis = v.ndim - 2
    low = (iota(v.shape, v.ndim - 1) & 4) == 0
    moved = jnp.where(low, pltpu.roll(lane_roll(v, -4), 1, axis), lane_roll(v, 4))
    return jnp.where(low & (iota(v.shape, axis) == 0), fill, moved)


def pair_after(v, fill):
    axis = v.ndim - 2
    high = (iota(v.shape, v.ndim - 1) & 4) != 0
    moved = jnp.where(high, pltpu.roll(lane_roll(v, 4), GX - 1, axis), lane_roll(v, -4))
    return jnp.where(high & (iota(v.shape, axis) == GX - 1), fill, moved)


def y_after(level, v, following):
    lane = iota(v.shape, v.ndim - 1)
    if level == 3:
        return jnp.where((lane & 3) == 3, lane_roll(following, 3), lane_roll(v, -1))
    return jnp.where((lane & 2) == 2, lane_roll(following, 2), lane_roll(v, -2))


def y_before(level, v, preceding):
    lane = iota(v.shape, v.ndim - 1)
    if level == 3:
        return jnp.where((lane & 3) == 0, lane_roll(preceding, -3), lane_roll(v, 1))
    return jnp.where((lane & 2) == 0, lane_roll(preceding, -2), lane_roll(v, 2))


def slots(shape):
    lane = iota(shape, len(shape) - 1)
    return (lane & 1) | ((lane >> 2) & 2)


def tiles_from_slots(parts):
    slot = slots(parts[0].shape)
    return jnp.where(slot == 0, parts[0], jnp.where(slot == 1, parts[1], jnp.where(slot == 2, parts[2], parts[3])))


def slot_after(v, fill):
    slot = slots(v.shape)
    return jnp.where(slot == 3, fill, jnp.where(slot == 1, lane_roll(v, -7), lane_roll(v, -1)))


def slot_before(v, fill):
    slot = slots(v.shape)
    return jnp.where(slot == 0, fill, jnp.where(slot == 2, lane_roll(v, 7), lane_roll(v, 1)))


def coarse_levels(f3, e3, s3, w3, v3, s4):
    lane = iota((C3, GX, LANES), 2)
    even3 = ((lane ^ (lane >> 3)) & 1) == 0
    z_last3 = (lane >> 3) == 15
    chunks = range(0, GY, C3)

    def face(scale, a, b):
        return (2.0 * scale) * a * b / (a + b)

    zero = jnp.zeros((GX, LANES), F32)
    for k in range(2):
        e3[k, 0] = lane_roll(e3[k, 1], 3)
        e3[k, 1 + GY] = lane_roll(e3[k, GY], -3)
        v3[k, 0] = zero
        v3[k, 1 + GY] = zero
    scale = 0.25**3
    e4 = []
    for g in chunks:
        here = pl.ds(1 + g, C3)
        both = (e3[0, here], e3[1, here])
        inner = face(scale, both[0], both[1])
        outer = (face(scale, both[0], pair_before(both[1], both[0])),
                 face(scale, both[1], pair_after(both[0], both[1])))
        yp, ym, zp, zm, f = [], [], [], [], []
        for r in range(2):
            own = both[r]
            yp.append(face(scale, own, y_after(3, own, e3[r, pl.ds(2 + g, C3)])))
            ym.append(face(scale, own, y_before(3, own, e3[r, pl.ds(g, C3)])))
            z = jnp.where(z_last3, 0.0, face(scale, own, lane_roll(own, -8)))
            zp.append(z)
            zm.append(lane_roll(z, 8))
            f.append(f3[r, pl.ds(g, C3)])
        for k in range(2):
            a, b = k, 1 - k
            parts = [jnp.where(even3, t[a], t[b]) for t in (outer, yp, ym, zp, zm)]
            weight_sum = inner
            for t in parts:
                weight_sum = weight_sum + t
            inverse = 1.0 / weight_sum
            source = jnp.where(even3, f[a], f[b]) * inverse
            s3[k, 0, pl.ds(g, C3)] = source
            s3[k, 1, pl.ds(g, C3)] = inner * inverse
            for i in range(5):
                s3[k, 2 + i, pl.ds(g, C3)] = parts[i] * inverse
            if k == 0:
                w3[pl.ds(g, C3)] = weight_sum
                v3[0, here] = source
        t = both[0] + both[1]
        t = t + flip(t, 1)
        e4.append((t + flip(t, 8)) * 0.125)

    def update3(k, g):
        o = 1 - k
        own = v3[o, pl.ds(1 + g, C3)]
        before, after = pair_before(own, 0.0), pair_after(own, 0.0)
        outer = jnp.where(even3, before, after) if k == 0 else jnp.where(even3, after, before)
        sides = (own, outer, y_after(3, own, v3[o, pl.ds(2 + g, C3)]),
                 y_before(3, own, v3[o, pl.ds(g, C3)]), lane_roll(own, -8), lane_roll(own, 8))
        part = [s3[k, 1 + i, pl.ds(g, C3)] * sides[i] for i in range(6)]
        return ((s3[k, 0, pl.ds(g, C3)] + part[0]) + (part[1] + part[2])) + ((part[3] + part[4]) + part[5])

    def sweep3(k):
        for g in chunks:
            v3[k, pl.ds(1 + g, C3)] = update3(k, g)

    sweep3(1)
    sweep3(0)
    sweep3(1)
    f4 = []
    for g in chunks:
        t = (update3(0, g) - v3[0, pl.ds(1 + g, C3)]) * w3[pl.ds(g, C3)]
        t = t + flip(t, 1)
        f4.append((t + flip(t, 8)) * 0.125)

    def regroup(parts):
        tiles = [part[i] for part in parts for i in range(C3)]
        return [tiles_from_slots(tiles[b::CHUNK]) for b in range(CHUNK)]

    e4, f4 = regroup(e4), regroup(f4)
    tile = (GX, LANES)
    lane = iota(tile, 1)
    even4 = (((lane >> 1) ^ (lane >> 2) ^ (lane >> 4)) & 1) == 0
    z_last4 = (lane >> 4) == 7
    scale = 0.25**4
    e_after = e4[1:] + [slot_after(e4[0], lane_roll(e4[-1], -2))]
    e_before = [slot_before(e4[-1], lane_roll(e4[0], 2))] + e4[:-1]
    v = []
    for b in range(CHUNK):
        own = e4[b]
        z = jnp.where(z_last4, 0.0, face(scale, own, lane_roll(own, -16)))
        parts = [face(scale, own, pair_before(own, own)), face(scale, own, pair_after(own, own)),
                 face(scale, own, y_after(4, own, e_after[b])), face(scale, own, y_before(4, own, e_before[b])),
                 z, lane_roll(z, 16)]
        weight_sum = parts[0]
        for t in parts[1:]:
            weight_sum = weight_sum + t
        inverse = 1.0 / weight_sum
        source = f4[b] * inverse
        s4[0, b] = source
        for i in range(6):
            s4[1 + i, b] = parts[i] * inverse
        v.append(jnp.where(even4, source, 0.0))

    def sweep4(k, v):
        v = list(v)
        after = v[1:] + [slot_after(v[0], 0.0)]
        before = [slot_before(v[-1], 0.0)] + v[:-1]
        new = []
        for b in range(CHUNK):
            own = v[b]
            x = s4[1, b] * pair_before(own, 0.0) + s4[2, b] * pair_after(own, 0.0)
            y = s4[3, b] * y_after(4, own, after[b]) + s4[4, b] * y_before(4, own, before[b])
            z = s4[5, b] * lane_roll(own, -16) + s4[6, b] * lane_roll(own, 16)
            value = (s4[0, b] + z) + (x + y)
            new.append(jnp.where(even4, value, own) if k == 0 else jnp.where(even4, own, value))
        return tuple(new)

    v = sweep4(1, v)
    if STOP >= 11:
        v = lax.fori_loop(0, COARSE_SWEEPS - 1, lambda i, v: sweep4(1, sweep4(0, v)), v)
    slot = slots(tile)
    for a in range(GY // CHUNK):
        for b in range(CHUNK):
            u = jnp.where(slot == a, v[b], 0.0)
            u = u + flip(u, 1)
            u = u + flip(u, 8)
            g = 1 + CHUNK * a + b
            v3[0, g] = v3[0, g] + u
            v3[1, g] = v3[1, g] + u
    if STOP < 12:
        return
    sweep3(0)
    sweep3(1)
    sweep3(0)
    sweep3(1)


def around_from_level3(v3, up, gx, gy):
    shape = (GX, LANES)
    lane, sub = iota(shape, 1), iota(shape, 0)
    even3 = ((lane ^ (lane >> 3)) & 1) == 0
    head = (lane & 7) == 0
    outside = ((sub == 0) & (gx == 0)) | ((sub == 2) & (gx == GX - 1))
    up[...] = jnp.zeros(up.shape, F32)
    for dy in range(3):
        red = v3[0, gy + dy]
        black = v3[1, gy + dy]
        for r in range(2):
            t = jnp.where(even3, red, black) if r == 0 else jnp.where(even3, black, red)
            t = jnp.where(outside, 0.0, pltpu.roll(t, lax.rem(GX + 1 - gx, GX), 0))
            for s in range(8):
                w = jnp.where(head, lane_roll(t, -s), 0.0)
                w = w + lane_roll(w, 1)
                w = w + lane_roll(w, 2)
                w = w + lane_roll(w, 4)
                for dx in range(3):
                    x = 4 * dx + 2 * (s // 4) + r
                    y = 4 + 2 * (4 * dy + s % 4)
                    up[x, y : y + 2, :] = jnp.broadcast_to(w[dx : dx + 1], (2, LANES))


def climb(near, far, s0, i0, s1, i1, s2, i2, out, f3, e3, s3, w3, v3, s4, v2, v1, v0,
          up3, up):
    gx, gy = lax.axis_index("gx"), lax.axis_index("gy")
    clear(v2, 32)
    clear(v1, 48)
    clear(v0, 48)
    for c, held in enumerate((near, far)):
        for dx in range(4):
            for dy in range(4):
                g = (((gy // 8 + dx) & 3) * 4 + ((gy // 2 + dy) & 3)) * 2 + (gy & 1 if c == 0 else 1 - (gy & 1))
                for r in range(2):
                    f3[r, g] = held[dx, dy, pl.ds(r, GX, stride=4), :]
                    e3[r, 1 + g] = held[dx, dy, pl.ds(2 + r, GX, stride=4), :]
    if STOP >= 10:
        coarse_levels(f3, e3, s3, w3, v3, s4)
    around_from_level3(v3, up3, gx, gy)

    if STOP >= 13:

        def add2(p):
            new = [i2[k, p, 8:40, :] + up3[p - 2] for k in range(2)]

            def store():
                for k in range(2):
                    v2[k, p, 8:40, :] = new[k]

            return store

        loop(2, 14, add2, UNROLL["add"])
        half_sweep(2, 0, 6, v2, s2)
        half_sweep(2, 1, 5, v2, s2)
        half_sweep(2, 0, 4, v2, s2)
        half_sweep(2, 1, 3, v2, s2)

    def raised(level, first, last, offset, coarse_v, v_in, v):
        def doubled(c):
            rows = 24
            even = pair_is_even(level + 1, rows)
            start = 8 + (12 if level == 0 else 4)
            red = coarse_v[0, c, start : start + rows, :]
            black = coarse_v[1, c, start : start + rows, :]
            both = (jnp.where(even, red, black), jnp.where(even, black, red))

            def store():
                for s in range(2):
                    for twice in range(2):
                        up[c, s, pl.ds(twice, rows, stride=2), :] = both[s]

            return store

        loop(first, last, doubled, 2)

        def add(c):
            new = [(k, 2 * c - offset + s, v_in[k, 2 * c - offset + s, 8:56, :] + up[c, s])
                   for s in range(2) for k in range(2)]

            def store():
                for k, p, value in new:
                    v[k, p, 8:56, :] = value

            return store

        loop(first, last, add, 1)

    if STOP >= 14:
        raised(1, 4, 12, 4, v2, i1, v1)
        half_sweep(1, 0, 5, v1, s1, (KEPT[0], KEPT[2]))
        half_sweep(1, 1, 4, v1, s1, (KEPT[0], KEPT[2]))
        half_sweep(1, 0, 3, v1, s1, (KEPT[0], KEPT[2]))
        half_sweep(1, 1, 2, v1, s1, (KEPT[0], KEPT[2]))

    if STOP >= 15:
        raised(0, 7, 17, 12, v1, i0, v0)
        half_sweep(0, 0, 3, v0, s0)
        half_sweep(0, 1, 2, v0, s0)
        half_sweep(0, 0, 1, v0, s0)
        half_sweep(0, 1, 0, v0, s0)
    even = pair_is_even(0, 32)

    def finish(q):
        red = v0[0, 4 + q, 16:48, :]
        black = v0[1, 4 + q, 16:48, :]

        def store():
            out[2 * q] = jnp.where(even, red, black)
            out[2 * q + 1] = jnp.where(even, black, red)

        return store

    loop(0, 16, finish, 4)


def shaped(*dims):
    return jax.ShapeDtypeStruct(dims, F32)


def kept_shapes(level):
    ext = EXT[level]
    kept = shaped(ext // 2, 2, 7, ext, LANES)
    if level == 1:
        kept = shaped(KEPT[1] - KEPT[0], 2, 7, KEPT[3] - KEPT[2], LANES)
    return kept, shaped(2, ext // 2, ext + 16, LANES)


def down_scratch(level):
    ext = EXT[level]
    vmem = [(ext + 2, ext + 16, LANES), (ext, ext, LANES), (ext // 2, ext, LANES), (2, 16, ext, LANES)]
    return [pltpu.VMEM(s, F32) for s in vmem]


def kernel_call(body, in_spaces, out_shape, out_spaces, scratch, mib, *operands):
    def specs(spaces):
        return [pl.BlockSpec(memory_space=pltpu.VMEM if s == "v" else pl.ANY) for s in spaces]

    return pl.pallas_call(
        body,
        in_specs=specs(in_spaces),
        out_specs=tuple(specs(out_spaces)),
        out_shape=tuple(out_shape),
        scratch_shapes=scratch,
        compiler_params=pltpu.CompilerParams(vmem_limit_bytes=mib << 20),
        name=body.__name__,
    )(*operands)


def exchange(axis, to_next, to_previous):
    count = lax.axis_size(axis)
    onward = [(i, (i + 1) % count) for i in range(count)]
    backward = [((i + 1) % count, i) for i in range(count)]
    return lax.ppermute(to_next, axis, onward), lax.ppermute(to_previous, axis, backward)


def from_offset(values, dx, dy, dc):
    moves = []
    for g in range(GY):
        x, y, c = g // 8, (g // 2) % 4, g % 2
        moves.append((((x + dx) % 4 * 4 + (y + dy) % 4) * 2 + (c ^ dc), g))
    return lax.ppermute(values, "gy", moves)


def per_device(right_side, permittivity):
    both = (right_side, permittivity)
    xl, xr = exchange("gx", jnp.stack([b[24:] for b in both]), jnp.stack([b[:8] for b in both]))
    yl, yr = exchange("gy", jnp.stack([b[:, 24:] for b in both]), jnp.stack([b[:, :8] for b in both]))
    xl, xr, yl, yr = lax.optimization_barrier((xl, xr, yl, yr))
    corners = jnp.concatenate([xl, xr], axis=1)
    cl, cr = exchange("gy", corners[:, :, 24:], corners[:, :, :8])
    p1, s0, v0 = kernel_call(
        down0, "aavvvvvv", (shaped(16, 16, LANES),) + kept_shapes(0), KEPT_SPEC,
        down_scratch(0) + [pltpu.SemaphoreType.DMA((18,))], 8,
        right_side, permittivity, xl, xr, yl, yr, cl, cr)

    xl, xr = exchange("gx", p1[3:], p1[:13])
    yl, yr = exchange("gy", p1, p1)
    xl, xr, yl, yr = lax.optimization_barrier((xl, xr, yl, yr))
    corners = jnp.concatenate([xl, xr], axis=0)
    cl, cr = exchange("gy", corners, corners)
    p2, s1, v1 = kernel_call(
        down1, "vvvvvvv", (shaped(16, 16, LANES),) + kept_shapes(1), "vav", down_scratch(1)
        + [pltpu.VMEM((EXT[1] // 2, 2, 7, EXT[1], LANES), F32), pltpu.SemaphoreType.DMA((GROUPS,))], 16,
        p1, xl, xr, yl, yr, cl, cr)

    xl, xr = exchange("gx", p2[:8], p2[8:])
    yl, yr = exchange("gy", p2[:, :8], p2[:, 8:])
    xl, xr, yl, yr = lax.optimization_barrier((xl, xr, yl, yr))
    corners = jnp.concatenate([xl, xr], axis=0)
    cl, cr = exchange("gy", corners[:, :8], corners[:, 8:])
    p3, s2, v2 = kernel_call(
        down2, "vvvvvvv", (shaped(GX, 4, LANES),) + kept_shapes(2), KEPT_SPEC,
        down_scratch(2) + [pltpu.VMEM((2, 4, 8, LANES), F32)], 8, p2, xl, xr, yl, yr, cl, cr)

    column = lax.all_to_all(p3, "gx", 0, 0, tiled=True).reshape(4 * GX, LANES)
    along_y = jnp.stack([column] + [from_offset(column, 0, d, 0) for d in (1, 2, 3)])
    near = jnp.stack([along_y] + [from_offset(along_y, d, 0, 0) for d in (1, 2, 3)])
    far = from_offset(near, 0, 0, 1)
    return climb_call(near, far, s0, v0, s1, v1, s2, v2)


def climb_call(*operands):
    rows = GY + 2
    vmem = [
        (2, GY, GX, LANES), (2, rows, GX, LANES), (2, 7, GY, GX, LANES), (GY, GX, LANES), (2, rows, GX, LANES),
        (7, CHUNK, GX, LANES),
        (2, 16, 48, LANES), (2, 24, 64, LANES), (2, 24, 64, LANES), (12, 32, LANES), (17, 2, 48, LANES),
    ]
    scratch = [pltpu.VMEM(s, F32) for s in vmem]
    return kernel_call(climb, "vvvvvvvv", (shaped(32, 32, LANES),), "v", scratch, 14, *operands)[0]


def solution(mesh):
    placed = (P("gx", "gy", None), P("gx", "gy", None))
    return jax.shard_map(
        per_device, mesh=mesh, in_specs=placed, out_specs=P("gx", "gy", None), check_vma=False
    )
```

```python
import jax
import jax.numpy as jnp
from jax import lax
from jax.experimental import pallas as pl
from jax.experimental.pallas import tpu as pltpu
from jax.sharding import PartitionSpec as P

F32 = jnp.float32
LANES = 128
COARSE_SWEEPS = 12
OWN = (32, 16, 8)
HALO = (8, 16, 12)
EXT = (48, 48, 32)
GX = 8
GY = 32
CHUNK = 8
KEPT = (5, 19, 8, 40)
GROUPS = 4


UNROLL = {"sweep": 6, "restrict": 4, "put": 16, "add": 4}
STOP = 99
KEPT_SPEC = "vvv"


def loop(first, last, body, step):
    def several(base, count):
        for store in [body(base + j) for j in range(count)]:
            store()

    whole = (last - first) // step
    if whole > 1:
        def one(i, carry):
            several(first + i * step, step)
            return carry

        lax.fori_loop(0, whole, one, 0)
    elif whole == 1:
        several(first, step)
    if (last - first) % step:
        several(first + whole * step, (last - first) % step)


def iota(shape, dim):
    return lax.broadcasted_iota(jnp.int32, shape, dim)


def lane_roll(v, shift):
    return pltpu.roll(v, shift % LANES, v.ndim - 1)


def flip(v, bit):
    lane = iota(v.shape, v.ndim - 1)
    return jnp.where((lane & bit) == 0, lane_roll(v, -bit), lane_roll(v, bit))


def pair_is_even(level, rows):
    shape = (rows, LANES)
    return ((iota(shape, 0) ^ (iota(shape, 1) >> level)) & 1) == 0


def bounds(level, index, count):
    own, halo, ext = OWN[level], HALO[level], EXT[level]
    low = halo - index * own
    high = halo + (count - index) * own
    return low, high


def clamp_edges(level, e, gx, gy):
    own, halo, ext = OWN[level], HALO[level], EXT[level]
    for back in range(-(-halo // own)):
        low = halo - back * own
        high = halo + own + back * own
        if low >= 1:

            @pl.when(gx == back)
            def _():
                e[low - 1] = e[low]

            @pl.when(gy == back)
            def _():
                e[0:ext, 8 + low - 1 : 8 + low, :] = e[0:ext, 8 + low : 8 + low + 1, :]

        if high < ext:

            @pl.when(gx == GX - 1 - back)
            def _():
                e[high] = e[high - 1]

            @pl.when(gy == GY - 1 - back)
            def _():
                e[0:ext, 8 + high : 8 + high + 1, :] = e[0:ext, 8 + high - 1 : 8 + high, :]


def faces(pairs):
    sums = [a + b for a, b in pairs]
    first = sums[0] * sums[1]
    whole = 1.0 / (first * sums[2])
    rest = whole * sums[2]
    inverse = (rest * sums[1], rest * sums[0], whole * first)
    return [a * b * i for (a, b), i in zip(pairs, inverse)]


def inverses(a, b):
    whole = 1.0 / (a * b)
    return whole * b, whole * a


def prepare(level, first, last, e, f, state, total, v, gx, gy, after_pair=None):
    ext = EXT[level]
    step = 1 << level
    source_scale = 0.5 * 4.0**level

    xlow, xhigh = bounds(level, gx, GX)
    ylow, yhigh = bounds(level, gy, GY)
    shape = (8, LANES)
    lane = iota(shape, 1)
    z_last = (lane >> level) == (LANES >> level) - 1
    even = pair_is_even(level, 8)
    aligned = all((HALO[level] + i * OWN[level]) % 8 == 0 for i in range(2))

    def tile(p, r, before, below):
        mid = slice(8 + r, 16 + r)
        up = slice(9 + r, 17 + r)
        e0 = e[2 * p, mid, :]
        e1 = e[2 * p + 1, mid, :]
        after = e[2 * p + 2, mid, :]
        outer0 = before
        inner, outer1, yp0 = faces(((e0, e1), (e1, after), (e0, e[2 * p, up, :])))
        yp1, zp0, zp1 = faces(((e1, e[2 * p + 1, up, :]), (e0, lane_roll(e0, -step)), (e1, lane_roll(e1, -step))))
        zp0 = jnp.where(z_last, 0.0, zp0)
        zp1 = jnp.where(z_last, 0.0, zp1)
        turned = pltpu.roll(yp0, 1, 0), pltpu.roll(yp1, 1, 0)
        if below is None:
            below = turned
        ym0, ym1 = (jnp.where(top, below[i], turned[i]) for i in range(2))
        zm0 = lane_roll(zp0, step)
        zm1 = lane_roll(zp1, step)
        f0 = f[2 * p, r : r + 8, :]
        f1 = f[2 * p + 1, r : r + 8, :]
        ok = (2 * p >= xlow) & (2 * p < xhigh)
        if aligned:
            ok = jnp.where(ok & (r >= ylow) & (r < yhigh), 1.0, 0.0)
        else:
            row = r + iota(shape, 0)
            ok = jnp.where(ok, 1.0, 0.0) * jnp.where((row >= ylow) & (row < yhigh), 1.0, 0.0)
        sides, sums = [], []
        for k in range(2):
            pick = even if k == 0 else jnp.logical_not(even)
            side = [inner] + [jnp.where(pick, a, b) for a, b in (
                (outer0, outer1), (yp0, yp1), (ym0, ym1), (zp0, zp1), (zm0, zm1))]
            sides.append(side)
            sums.append((side[0] + side[1]) + (side[2] + side[3]) + (side[4] + side[5]))
        inverse = inverses(*sums)
        for k in range(2):
            scaled = inverse[k] * ok
            source = (jnp.where(even, f0, f1) if k == 0 else jnp.where(even, f1, f0)) * (scaled * source_scale)
            state[p, k, 0, r : r + 8, :] = source
            for i in range(6):
                state[p, k, 1 + i, r : r + 8, :] = sides[k][i] * scaled
            if k == 0:
                total[p, r : r + 8, :] = sums[0]
                v[0, p, mid, :] = source
        return outer1, turned

    top = iota(shape, 0) == 0

    def body(p, carry):
        new, turned = [], None
        for c in range(ext // 8):
            outer, turned = tile(p, 8 * c, carry[c], turned)
            new.append(outer)
        if after_pair is not None:
            after_pair(p)
        return tuple(new)

    start = max(2 * first - 1, 0)
    init = []
    for c in range(ext // 8):
        a, b = e[start, 8 + 8 * c : 16 + 8 * c, :], e[2 * first, 8 + 8 * c : 16 + 8 * c, :]
        init.append(a * b / (a + b))
    init = tuple(init)
    lax.fori_loop(first, last, body, init)


def clear(v, ext):
    def body(p, carry):
        for j in range(4):
            for k in range(2):
                v[k, 4 * p + j] = jnp.zeros((ext + 16, LANES), F32)
        return carry

    lax.fori_loop(0, ext // 8, body, 0)


def updated(level, k, p, v, state, low, high, base=(0, 0)):
    step = 1 << level
    even = pair_is_even(level, high - low)
    mid = slice(8 + low, 8 + high)
    other = 1 - k
    here = v[other, p, mid, :]
    before = v[other, p - 1, mid, :]
    after = v[other, p + 1, mid, :]
    outer = jnp.where(even, before, after) if k == 0 else jnp.where(even, after, before)
    rows = slice(low - base[1], high - base[1])
    part = [state[p - base[0], k, 1 + i, rows, :] for i in range(6)]
    x = part[0] * here + part[1] * outer
    y = part[2] * v[other, p, 9 + low : 9 + high, :] + part[3] * v[other, p, 7 + low : 7 + high, :]
    z = part[4] * lane_roll(here, -step) + part[5] * lane_roll(here, step)
    return (state[p - base[0], k, 0, rows, :] + x) + (y + z)


def half_sweep(level, k, reach, v, state, base=(0, 0)):
    own, halo, ext = OWN[level], HALO[level], EXT[level]
    first = (halo - reach) // 2
    last = (halo + own + reach + 1) // 2
    low = (halo - reach) // 8 * 8
    high = -(-(halo + own + reach) // 8) * 8

    def body(p):
        value = updated(level, k, p, v, state, low, high, base)

        def store():
            v[k, p, 8 + low : 8 + high, :] = value

        return store

    loop(first, last, body, UNROLL["sweep"])


def restrict(level, first, pairs, row, count, v, state, total, e, tmp, put):
    step = 1 << level
    low = row // 8 * 8
    high = -(-(row + 2 * count) // 8) * 8
    mid = slice(8 + low, 8 + high)

    def fine(q):
        p = first + q
        residual = (updated(level, 0, p, v, state, low, high) - v[0, p, mid, :]) * total[p, low:high, :]
        both = e[2 * p, mid, :] + e[2 * p + 1, mid, :]

        def store():
            tmp[0, q, low:high, :] = residual
            tmp[1, q, low:high, :] = both

        return store

    def coarse(q):
        out = []
        for i in range(2):
            a = tmp[i, q, pl.ds(row, count, stride=2), :] + tmp[i, q, pl.ds(row + 1, count, stride=2), :]
            out.append((a + flip(a, step)) * (0.125 if i else 0.25 * 0.25**level))
        return lambda: put(q, out[0], out[1])

    loop(0, pairs, fine, UNROLL["restrict"])
    loop(0, pairs, coarse, 2 * UNROLL["restrict"])


def interleave(f, e):
    return jnp.where((iota(f.shape, f.ndim - 1) & 1) == 0, f, e)


def split(both):
    low = (iota(both.shape, both.ndim - 1) & 1) == 0
    return jnp.where(low, both, lane_roll(both, 1)), jnp.where(low, lane_roll(both, -1), both)


def fill_rim(e, ext):
    e[ext : ext + 2] = jnp.ones((2, ext + 16, LANES), F32)
    e[0:ext, 0:8, :] = jnp.ones((ext, 8, LANES), F32)
    e[0:ext, 8 + ext :, :] = jnp.ones((ext, 8, LANES), F32)


def start_all(copies):
    for copy in copies:
        copy.start()


def wait_all(copies):
    for copy in copies:
        copy.wait()


def sweep_down(level, pairs, reaches, inner, e, f, state, v, total, tmp, gx, gy, put, after_pair=None):
    clamp_edges(level, e, gx, gy)
    prepare(level, pairs[0], pairs[1], e, f, state, total, v, gx, gy, after_pair)
    if STOP >= 2:
        half_sweep(level, 1, reaches[0], v, state)
        half_sweep(level, 0, reaches[1], v, state)
        half_sweep(level, 1, reaches[2], v, state)
    if STOP >= 3:
        restrict(level, *inner, v, state, total, e, tmp, put)


def down0(f_in, e_in, xl, xr, yl, yr, cl, cr, out, state, v, e, f, total, tmp, in_sems):
    gx, gy = lax.axis_index("gx"), lax.axis_index("gy")
    ya, yb = 0, 40
    copies = []
    for i, (target, own, off) in enumerate(((f, f_in, 0), (e, e_in, 8))):
        parts = (
            (xl.at[i], target.at[pl.ds(0, 8), pl.ds(off + 8, 32)]),
            (own, target.at[pl.ds(8, 32), pl.ds(off + 8, 32)]),
            (xr.at[i], target.at[pl.ds(40, 8), pl.ds(off + 8, 32)]),
            (yl.at[i], target.at[pl.ds(8, 32), pl.ds(off + ya, 8)]),
            (yr.at[i], target.at[pl.ds(8, 32), pl.ds(off + yb, 8)]),
            (cl.at[i, pl.ds(0, 8)], target.at[pl.ds(0, 8), pl.ds(off + ya, 8)]),
            (cl.at[i, pl.ds(8, 8)], target.at[pl.ds(40, 8), pl.ds(off + ya, 8)]),
            (cr.at[i, pl.ds(0, 8)], target.at[pl.ds(0, 8), pl.ds(off + yb, 8)]),
            (cr.at[i, pl.ds(8, 8)], target.at[pl.ds(40, 8), pl.ds(off + yb, 8)]),
        )
        for j, (source, to) in enumerate(parts):
            copies.append(pltpu.make_async_copy(source, to, in_sems.at[9 * i + j]))
    start_all(copies)
    fill_rim(e, 48)
    clear(v, 48)
    wait_all(copies)

    def put(q, fc, ec):
        out[q] = interleave(fc, ec)

    if STOP >= 1:
        sweep_down(0, (0, 24), (6, 5, 4), (4, 16, 8, 16), e, f, state, v, total, tmp, gx, gy, put)


def put_split(source, start, count, x, y, e, f):
    height = source.shape[1]

    def body(i):
        fi, ei = split(source[start + i])

        def store():
            f[x + i, pl.ds(y, height), :] = fi
            e[x + i, pl.ds(8 + y, height), :] = ei

        return store

    loop(0, count, body, UNROLL["put"])


def down1(own, xl, xr, yl, yr, out, kept, v, e, f, total, tmp, state, sems):
    gx, gy = lax.axis_index("gx"), lax.axis_index("gy")
    fill_rim(e, 48)
    clear(v, 48)
    put_split(xl, 0, 13, 3, 16, e, f)
    put_split(own, 0, 16, 16, 16, e, f)
    put_split(xr, 0, 13, 32, 16, e, f)
    put_split(yl, 0, 42, 3, 0, e, f)
    put_split(yr, 0, 42, 3, 32, e, f)

    def put(q, fc, ec):
        out[q] = interleave(fc, ec)

    first, last, low, high = KEPT
    copies = []
    for g in range(GROUPS):
        a = first + (last - first) * g // GROUPS
        b = first + (last - first) * (g + 1) // GROUPS
        copies.append((b - 1, pltpu.make_async_copy(
            state.at[pl.ds(a, b - a), :, :, pl.ds(low, high - low), :], kept.at[pl.ds(a - first, b - a)], sems.at[g])))

    def after_pair(p):
        for end, copy in copies:

            @pl.when(p == end)
            def _():
                copy.start()

    sweep_down(1, (2, 22), (11, 10, 9), (4, 16, 8, 16), e, f, state, v, total, tmp, gx, gy, put, after_pair)
    wait_all([copy for _, copy in copies])


def down2(own, xl, xr, yl, yr, out, state, v, e, f, total, tmp, coarse):
    gx, gy = lax.axis_index("gx"), lax.axis_index("gy")
    fill_rim(e, 32)
    clear(v, 32)
    put_split(xl, 0, 8, 0, 8, e, f)
    put_split(own, 0, 16, 8, 8, e, f)
    put_split(xr, 0, 8, 24, 8, e, f)
    put_split(yl, 0, 32, 0, 0, e, f)
    put_split(yr, 0, 32, 0, 24, e, f)

    def put(q, fc, ec):
        coarse[0, q, 0:4, :] = fc
        coarse[1, q, 0:4, :] = ec

    if STOP >= 1:
        sweep_down(2, (1, 15), (9, 8, 7), (6, 4, 12, 4), e, f, state, v, total, tmp, gx, gy, put)
    slot = iota((1, LANES), 1) & 7
    for i in range(2):
        for r in range(2):
            row = jnp.zeros((1, LANES), F32)
            for x1 in range(2):
                for y in range(4):
                    row = jnp.where(slot == 4 * x1 + y, coarse[i, 2 * x1 + r, y : y + 1, :], row)
            out[:, 2 * i + r : 2 * i + r + 1, :] = jnp.broadcast_to(row[None], (GX, 1, LANES))


BLOCK = (CHUNK, GX, LANES)


def pair_before(v, fill):
    axis = v.ndim - 2
    low = (iota(v.shape, v.ndim - 1) & 4) == 0
    moved = jnp.where(low, pltpu.roll(lane_roll(v, -4), 1, axis), lane_roll(v, 4))
    return jnp.where(low & (iota(v.shape, axis) == 0), fill, moved)


def pair_after(v, fill):
    axis = v.ndim - 2
    high = (iota(v.shape, v.ndim - 1) & 4) != 0
    moved = jnp.where(high, pltpu.roll(lane_roll(v, 4), GX - 1, axis), lane_roll(v, -4))
    return jnp.where(high & (iota(v.shape, axis) == GX - 1), fill, moved)


def y_after(level, v, following):
    lane = iota(v.shape, v.ndim - 1)
    if level == 3:
        return jnp.where((lane & 3) == 3, lane_roll(following, 3), lane_roll(v, -1))
    return jnp.where((lane & 2) == 2, lane_roll(following, 2), lane_roll(v, -2))


def y_before(level, v, preceding):
    lane = iota(v.shape, v.ndim - 1)
    if level == 3:
        return jnp.where((lane & 3) == 0, lane_roll(preceding, -3), lane_roll(v, 1))
    return jnp.where((lane & 2) == 0, lane_roll(preceding, -2), lane_roll(v, 2))


def slots(shape):
    lane = iota(shape, len(shape) - 1)
    return (lane & 1) | ((lane >> 2) & 2)


def tiles_from_slots(parts):
    slot = slots(parts[0].shape)
    return jnp.where(slot == 0, parts[0], jnp.where(slot == 1, parts[1], jnp.where(slot == 2, parts[2], parts[3])))


def slot_after(v, fill):
    slot = slots(v.shape)
    return jnp.where(slot == 3, fill, jnp.where(slot == 1, lane_roll(v, -7), lane_roll(v, -1)))


def slot_before(v, fill):
    slot = slots(v.shape)
    return jnp.where(slot == 0, fill, jnp.where(slot == 2, lane_roll(v, 7), lane_roll(v, 1)))


def coarse_levels(f3, e3, s3, w3, v3, s4):
    tile = (GX, LANES)
    lane = iota(tile, 1)
    even3 = ((lane ^ (lane >> 3)) & 1) == 0
    z_last3 = (lane >> 3) == 15
    zero = jnp.zeros(tile, F32)
    everywhere = range(GY)

    def face(scale, a, b):
        return (2.0 * scale) * a * b / (a + b)

    e = [[e3[r, g] for g in everywhere] for r in range(2)]
    after = [e[r][1:] + [lane_roll(e[r][-1], -3)] for r in range(2)]
    before = [[lane_roll(e[r][0], 3)] + e[r][:-1] for r in range(2)]
    red, e4 = [], []
    for g in everywhere:
        both = (e[0][g], e[1][g])
        inner, outer0, outer1 = faces((
            both, (both[0], pair_before(both[1], both[0])), (both[1], pair_after(both[0], both[1]))))
        yp, ym, zp, zm = [], [], [], []
        for r in range(2):
            own = both[r]
            up, down, z = faces((
                (own, y_after(3, own, after[r][g])), (own, y_before(3, own, before[r][g])), (own, lane_roll(own, -8))))
            z = jnp.where(z_last3, 0.0, z)
            yp.append(up)
            ym.append(down)
            zp.append(z)
            zm.append(lane_roll(z, 8))
        f = (f3[0, g], f3[1, g])
        sides, sums = [], []
        for k in range(2):
            side = [inner] + [jnp.where(even3, t[k], t[1 - k]) for t in ((outer0, outer1), yp, ym, zp, zm)]
            sides.append(side)
            sums.append((side[0] + side[1]) + (side[2] + side[3]) + (side[4] + side[5]))
        inverse = inverses(*sums)
        for k in range(2):
            source = jnp.where(even3, f[k], f[1 - k]) * (inverse[k] * (0.5 * 4.0**3))
            s3[k, 0, g] = source
            for i in range(6):
                s3[k, 1 + i, g] = sides[k][i] * inverse[k]
            if k == 0:
                w3[g] = sums[0]
                red.append(source)
        t = both[0] + both[1]
        t = t + flip(t, 1)
        e4.append((t + flip(t, 8)) * 0.125)

    def update3(k, other, g):
        own = other[g]
        following = other[g + 1] if g + 1 < GY else zero
        preceding = other[g - 1] if g else zero
        low, high = pair_before(own, 0.0), pair_after(own, 0.0)
        outer = jnp.where(even3, low, high) if k == 0 else jnp.where(even3, high, low)
        sides = (own, outer, y_after(3, own, following), y_before(3, own, preceding),
                 lane_roll(own, -8), lane_roll(own, 8))
        part = [s3[k, 1 + i, g] * sides[i] for i in range(6)]
        return ((s3[k, 0, g] + part[0]) + (part[1] + part[2])) + ((part[3] + part[4]) + part[5])

    def sweep3(k, other):
        return [update3(k, other, g) for g in everywhere]

    black = sweep3(1, red)
    red = sweep3(0, black)
    black = sweep3(1, red)
    f4 = []
    for g in everywhere:
        t = (update3(0, black, g) - red[g]) * w3[g]
        t = t + flip(t, 1)
        f4.append((t + flip(t, 8)) * (0.25 * 0.25**3))

    def regroup(parts):
        return [tiles_from_slots(parts[b::CHUNK]) for b in range(CHUNK)]

    e4, f4 = regroup(e4), regroup(f4)
    tile = (GX, LANES)
    lane = iota(tile, 1)
    even4 = (((lane >> 1) ^ (lane >> 2) ^ (lane >> 4)) & 1) == 0
    z_last4 = (lane >> 4) == 7
    scale = 0.25**4
    e_after = e4[1:] + [slot_after(e4[0], lane_roll(e4[-1], -2))]
    e_before = [slot_before(e4[-1], lane_roll(e4[0], 2))] + e4[:-1]
    v = []
    for b in range(CHUNK):
        own = e4[b]
        z = jnp.where(z_last4, 0.0, face(scale, own, lane_roll(own, -16)))
        parts = [face(scale, own, pair_before(own, own)), face(scale, own, pair_after(own, own)),
                 face(scale, own, y_after(4, own, e_after[b])), face(scale, own, y_before(4, own, e_before[b])),
                 z, lane_roll(z, 16)]
        weight_sum = parts[0]
        for t in parts[1:]:
            weight_sum = weight_sum + t
        inverse = 1.0 / weight_sum
        source = f4[b] * inverse
        s4[0, b] = source
        for i in range(6):
            s4[1 + i, b] = parts[i] * inverse
        v.append(jnp.where(even4, source, 0.0))

    def sweep4(k, v):
        v = list(v)
        after = v[1:] + [slot_after(v[0], 0.0)]
        before = [slot_before(v[-1], 0.0)] + v[:-1]
        new = []
        for b in range(CHUNK):
            own = v[b]
            x = s4[1, b] * pair_before(own, 0.0) + s4[2, b] * pair_after(own, 0.0)
            y = s4[3, b] * y_after(4, own, after[b]) + s4[4, b] * y_before(4, own, before[b])
            z = s4[5, b] * lane_roll(own, -16) + s4[6, b] * lane_roll(own, 16)
            value = (s4[0, b] + z) + (x + y)
            new.append(jnp.where(even4, value, own) if k == 0 else jnp.where(even4, own, value))
        return tuple(new)

    v = sweep4(1, v)
    if STOP >= 11:
        v = lax.fori_loop(0, COARSE_SWEEPS - 1, lambda i, v: sweep4(1, sweep4(0, v)), v)
    slot = slots(tile)
    for a in range(GY // CHUNK):
        for b in range(CHUNK):
            u = jnp.where(slot == a, v[b], 0.0)
            u = u + flip(u, 1)
            u = u + flip(u, 8)
            g = CHUNK * a + b
            red[g] = red[g] + u
            black[g] = black[g] + u
    for _ in range(2):
        red = sweep3(0, black)
        black = sweep3(1, red)
    for k, values in enumerate((red, black)):
        v3[k, 0] = zero
        v3[k, 1 + GY] = zero
        for g in everywhere:
            v3[k, 1 + g] = values[g]


def around_from_level3(v3, up, gx, gy):
    shape = (GX, LANES)
    lane, sub = iota(shape, 1), iota(shape, 0)
    even3 = ((lane ^ (lane >> 3)) & 1) == 0
    head = (lane & 7) == 0
    outside = ((sub == 0) & (gx == 0)) | ((sub == 2) & (gx == GX - 1))
    up[...] = jnp.zeros(up.shape, F32)
    for dy in range(3):
        red = v3[0, gy + dy]
        black = v3[1, gy + dy]
        for r in range(2):
            t = jnp.where(even3, red, black) if r == 0 else jnp.where(even3, black, red)
            t = jnp.where(outside, 0.0, pltpu.roll(t, lax.rem(GX + 1 - gx, GX), 0))
            for s in range(8):
                w = jnp.where(head, lane_roll(t, -s), 0.0)
                w = w + lane_roll(w, 1)
                w = w + lane_roll(w, 2)
                w = w + lane_roll(w, 4)
                for dx in range(3):
                    x = 4 * dx + 2 * (s // 4) + r
                    y = 4 + 2 * (4 * dy + s % 4)
                    up[x, y : y + 2, :] = jnp.broadcast_to(w[dx : dx + 1], (2, LANES))


def climb(near, far, s0, i0, s1, i1, s2, i2, out, f3, e3, s3, w3, v3, s4, v2, v1, v0,
          up3, up):
    gx, gy = lax.axis_index("gx"), lax.axis_index("gy")
    clear(v2, 32)
    clear(v1, 48)
    clear(v0, 48)
    for c, held in enumerate((near, far)):
        for dx in range(4):
            for dy in range(4):
                g = (((gy // 8 + dx) & 3) * 4 + ((gy // 2 + dy) & 3)) * 2 + (gy & 1 if c == 0 else 1 - (gy & 1))
                for r in range(2):
                    f3[r, g] = held[dx, dy, pl.ds(r, GX, stride=4), :]
                    e3[r, g] = held[dx, dy, pl.ds(2 + r, GX, stride=4), :]
    if STOP >= 10:
        coarse_levels(f3, e3, s3, w3, v3, s4)
    around_from_level3(v3, up3, gx, gy)

    if STOP >= 13:

        def add2(p):
            new = [i2[k, p, 8:40, :] + up3[p - 2] for k in range(2)]

            def store():
                for k in range(2):
                    v2[k, p, 8:40, :] = new[k]

            return store

        loop(2, 14, add2, UNROLL["add"])
        half_sweep(2, 0, 6, v2, s2)
        half_sweep(2, 1, 5, v2, s2)
        half_sweep(2, 0, 4, v2, s2)
        half_sweep(2, 1, 3, v2, s2)

    def raised(level, first, last, offset, coarse_v, v_in, v):
        def doubled(c):
            rows = 24
            even = pair_is_even(level + 1, rows)
            start = 8 + (12 if level == 0 else 4)
            red = coarse_v[0, c, start : start + rows, :]
            black = coarse_v[1, c, start : start + rows, :]
            both = (jnp.where(even, red, black), jnp.where(even, black, red))

            def store():
                for s in range(2):
                    for twice in range(2):
                        up[c, s, pl.ds(twice, rows, stride=2), :] = both[s]

            return store

        loop(first, last, doubled, 2)

        def add(c):
            new = [(k, 2 * c - offset + s, v_in[k, 2 * c - offset + s, 8:56, :] + up[c, s])
                   for s in range(2) for k in range(2)]

            def store():
                for k, p, value in new:
                    v[k, p, 8:56, :] = value

            return store

        loop(first, last, add, 1)

    if STOP >= 14:
        raised(1, 4, 12, 4, v2, i1, v1)
        half_sweep(1, 0, 5, v1, s1, (KEPT[0], KEPT[2]))
        half_sweep(1, 1, 4, v1, s1, (KEPT[0], KEPT[2]))
        half_sweep(1, 0, 3, v1, s1, (KEPT[0], KEPT[2]))
        half_sweep(1, 1, 2, v1, s1, (KEPT[0], KEPT[2]))

    if STOP >= 15:
        raised(0, 7, 17, 12, v1, i0, v0)
        half_sweep(0, 0, 3, v0, s0)
        half_sweep(0, 1, 2, v0, s0)
        half_sweep(0, 0, 1, v0, s0)
        half_sweep(0, 1, 0, v0, s0)
    even = pair_is_even(0, 32)

    def finish(q):
        red = v0[0, 4 + q, 16:48, :]
        black = v0[1, 4 + q, 16:48, :]

        def store():
            out[2 * q] = jnp.where(even, red, black)
            out[2 * q + 1] = jnp.where(even, black, red)

        return store

    loop(0, 16, finish, 4)


def shaped(*dims):
    return jax.ShapeDtypeStruct(dims, F32)


def kept_shapes(level):
    ext = EXT[level]
    kept = shaped(ext // 2, 2, 7, ext, LANES)
    if level == 1:
        kept = shaped(KEPT[1] - KEPT[0], 2, 7, KEPT[3] - KEPT[2], LANES)
    return kept, shaped(2, ext // 2, ext + 16, LANES)


def down_scratch(level):
    ext = EXT[level]
    vmem = [(ext + 2, ext + 16, LANES), (ext, ext, LANES), (ext // 2, ext, LANES), (2, 16, ext, LANES)]
    return [pltpu.VMEM(s, F32) for s in vmem]


def kernel_call(body, in_spaces, out_shape, out_spaces, scratch, mib, *operands):
    def specs(spaces):
        return [pl.BlockSpec(memory_space=pltpu.VMEM if s == "v" else pl.ANY) for s in spaces]

    return pl.pallas_call(
        body,
        in_specs=specs(in_spaces),
        out_specs=tuple(specs(out_spaces)),
        out_shape=tuple(out_shape),
        scratch_shapes=scratch,
        compiler_params=pltpu.CompilerParams(vmem_limit_bytes=mib << 20),
        name=body.__name__,
    )(*operands)


def exchange(axis, to_next, to_previous):
    count = lax.axis_size(axis)
    onward = [(i, (i + 1) % count) for i in range(count)]
    backward = [((i + 1) % count, i) for i in range(count)]
    return lax.ppermute(to_next, axis, onward), lax.ppermute(to_previous, axis, backward)


def from_offset(values, dx, dy, dc):
    moves = []
    for g in range(GY):
        x, y, c = g // 8, (g // 2) % 4, g % 2
        moves.append((((x + dx) % 4 * 4 + (y + dy) % 4) * 2 + (c ^ dc), g))
    return lax.ppermute(values, "gy", moves)


def per_device(right_side, permittivity):
    both = (right_side, permittivity)
    xl, xr = exchange("gx", jnp.stack([b[24:] for b in both]), jnp.stack([b[:8] for b in both]))
    yl, yr = exchange("gy", jnp.stack([b[:, 24:] for b in both]), jnp.stack([b[:, :8] for b in both]))
    corners = jnp.concatenate([xl, xr], axis=1)
    cl, cr = exchange("gy", corners[:, :, 24:], corners[:, :, :8])
    p1, s0, v0 = kernel_call(
        down0, "aavvvvvv", (shaped(16, 16, LANES),) + kept_shapes(0), KEPT_SPEC,
        down_scratch(0) + [pltpu.SemaphoreType.DMA((18,))], 8,
        right_side, permittivity, xl, xr, yl, yr, cl, cr)

    xl, xr = exchange("gx", p1[3:], p1[:13])
    wide = jnp.concatenate([xl, p1, xr], axis=0)
    yl, yr = exchange("gy", wide, wide)
    p2, s1, v1 = kernel_call(
        down1, "vvvvv", (shaped(16, 16, LANES),) + kept_shapes(1), "vav", down_scratch(1)
        + [pltpu.VMEM((EXT[1] // 2, 2, 7, EXT[1], LANES), F32), pltpu.SemaphoreType.DMA((GROUPS,))], 16,
        p1, xl, xr, yl, yr)

    xl, xr = exchange("gx", p2[:8], p2[8:])
    wide = jnp.concatenate([xl, p2, xr], axis=0)
    yl, yr = exchange("gy", wide[:, :8], wide[:, 8:])
    p3, s2, v2 = kernel_call(
        down2, "vvvvv", (shaped(GX, 4, LANES),) + kept_shapes(2), KEPT_SPEC,
        down_scratch(2) + [pltpu.VMEM((2, 4, 8, LANES), F32)], 8, p2, xl, xr, yl, yr)

    column = lax.all_to_all(p3, "gx", 0, 0, tiled=True).reshape(4 * GX, LANES)
    along_y = jnp.stack([column] + [from_offset(column, 0, d, 0) for d in (1, 2, 3)])
    near = jnp.stack([along_y] + [from_offset(along_y, d, 0, 0) for d in (1, 2, 3)])
    far = from_offset(near, 0, 0, 1)
    return climb_call(near, far, s0, v0, s1, v1, s2, v2)


def climb_call(*operands):
    rows = GY + 2
    vmem = [
        (2, GY, GX, LANES), (2, rows, GX, LANES), (2, 7, GY, GX, LANES), (GY, GX, LANES), (2, rows, GX, LANES),
        (7, CHUNK, GX, LANES),
        (2, 16, 48, LANES), (2, 24, 64, LANES), (2, 24, 64, LANES), (12, 32, LANES), (17, 2, 48, LANES),
    ]
    scratch = [pltpu.VMEM(s, F32) for s in vmem]
    return kernel_call(climb, "vvvvvvvv", (shaped(32, 32, LANES),), "v", scratch, 14, *operands)[0]


def solution(mesh):
    placed = (P("gx", "gy", None), P("gx", "gy", None))
    return jax.shard_map(
        per_device, mesh=mesh, in_specs=placed, out_specs=P("gx", "gy", None), check_vma=False
    )
```

```python
import jax
import jax.numpy as jnp
from jax import lax
from jax.experimental import pallas as pl
from jax.experimental.pallas import tpu as pltpu
from jax.sharding import PartitionSpec as P

F32 = jnp.float32
LANES = 128
COARSE_SWEEPS = 12
OWN = (32, 16, 8)
HALO = (8, 16, 12)
EXT = (48, 48, 32)
GX = 8
GY = 32
CHUNK = 8
C3 = 8
KEPT = (5, 19, 8, 40)
GROUPS = 4


UNROLL = {"sweep": 6, "restrict": 4, "put": 16, "add": 4}
STOP = 99
KEPT_SPEC = "vvv"


def loop(first, last, body, step):
    def several(base, count):
        for store in [body(base + j) for j in range(count)]:
            store()

    whole = (last - first) // step
    if whole > 1:
        def one(i, carry):
            several(first + i * step, step)
            return carry

        lax.fori_loop(0, whole, one, 0)
    elif whole == 1:
        several(first, step)
    if (last - first) % step:
        several(first + whole * step, (last - first) % step)


def iota(shape, dim):
    return lax.broadcasted_iota(jnp.int32, shape, dim)


def lane_roll(v, shift):
    return pltpu.roll(v, shift % LANES, v.ndim - 1)


def flip(v, bit):
    lane = iota(v.shape, v.ndim - 1)
    return jnp.where((lane & bit) == 0, lane_roll(v, -bit), lane_roll(v, bit))


def pair_is_even(level, rows):
    shape = (rows, LANES)
    return ((iota(shape, 0) ^ (iota(shape, 1) >> level)) & 1) == 0


def bounds(level, index, count):
    own, halo, ext = OWN[level], HALO[level], EXT[level]
    low = halo - index * own
    high = halo + (count - index) * own
    return low, high


def clamp_edges(level, e, gx, gy):
    own, halo, ext = OWN[level], HALO[level], EXT[level]
    for back in range(-(-halo // own)):
        low = halo - back * own
        high = halo + own + back * own
        if low >= 1:

            @pl.when(gx == back)
            def _():
                e[low - 1] = e[low]

            @pl.when(gy == back)
            def _():
                e[0:ext, 8 + low - 1 : 8 + low, :] = e[0:ext, 8 + low : 8 + low + 1, :]

        if high < ext:

            @pl.when(gx == GX - 1 - back)
            def _():
                e[high] = e[high - 1]

            @pl.when(gy == GY - 1 - back)
            def _():
                e[0:ext, 8 + high : 8 + high + 1, :] = e[0:ext, 8 + high - 1 : 8 + high, :]


def faces(pairs):
    sums = [a + b for a, b in pairs]
    first = sums[0] * sums[1]
    whole = 1.0 / (first * sums[2])
    rest = whole * sums[2]
    inverse = (rest * sums[1], rest * sums[0], whole * first)
    return [a * b * i for (a, b), i in zip(pairs, inverse)]


def inverses(a, b):
    whole = 1.0 / (a * b)
    return whole * b, whole * a


def prepare(level, first, last, e, f, state, total, v, gx, gy, after_pair=None):
    ext = EXT[level]
    step = 1 << level
    source_scale = 0.5 * 4.0**level

    xlow, xhigh = bounds(level, gx, GX)
    ylow, yhigh = bounds(level, gy, GY)
    shape = (8, LANES)
    lane = iota(shape, 1)
    z_last = (lane >> level) == (LANES >> level) - 1
    even = pair_is_even(level, 8)
    aligned = all((HALO[level] + i * OWN[level]) % 8 == 0 for i in range(2))

    def tile(p, r, before, below):
        mid = slice(8 + r, 16 + r)
        up = slice(9 + r, 17 + r)
        e0 = e[2 * p, mid, :]
        e1 = e[2 * p + 1, mid, :]
        after = e[2 * p + 2, mid, :]
        outer0 = before
        inner, outer1, yp0 = faces(((e0, e1), (e1, after), (e0, e[2 * p, up, :])))
        yp1, zp0, zp1 = faces(((e1, e[2 * p + 1, up, :]), (e0, lane_roll(e0, -step)), (e1, lane_roll(e1, -step))))
        zp0 = jnp.where(z_last, 0.0, zp0)
        zp1 = jnp.where(z_last, 0.0, zp1)
        turned = pltpu.roll(yp0, 1, 0), pltpu.roll(yp1, 1, 0)
        if below is None:
            below = turned
        ym0, ym1 = (jnp.where(top, below[i], turned[i]) for i in range(2))
        zm0 = lane_roll(zp0, step)
        zm1 = lane_roll(zp1, step)
        f0 = f[2 * p, r : r + 8, :]
        f1 = f[2 * p + 1, r : r + 8, :]
        ok = (2 * p >= xlow) & (2 * p < xhigh)
        if aligned:
            ok = jnp.where(ok & (r >= ylow) & (r < yhigh), 1.0, 0.0)
        else:
            row = r + iota(shape, 0)
            ok = jnp.where(ok, 1.0, 0.0) * jnp.where((row >= ylow) & (row < yhigh), 1.0, 0.0)
        sides, sums = [], []
        for k in range(2):
            pick = even if k == 0 else jnp.logical_not(even)
            side = [inner] + [jnp.where(pick, a, b) for a, b in (
                (outer0, outer1), (yp0, yp1), (ym0, ym1), (zp0, zp1), (zm0, zm1))]
            sides.append(side)
            sums.append((side[0] + side[1]) + (side[2] + side[3]) + (side[4] + side[5]))
        inverse = inverses(*sums)
        for k in range(2):
            scaled = inverse[k] * ok
            source = (jnp.where(even, f0, f1) if k == 0 else jnp.where(even, f1, f0)) * (scaled * source_scale)
            state[p, k, 0, r : r + 8, :] = source
            for i in range(6):
                state[p, k, 1 + i, r : r + 8, :] = sides[k][i] * scaled
            if k == 0:
                total[p, r : r + 8, :] = sums[0]
                v[0, p, mid, :] = source
        return outer1, turned

    top = iota(shape, 0) == 0

    def body(p, carry):
        new, turned = [], None
        for c in range(ext // 8):
            outer, turned = tile(p, 8 * c, carry[c], turned)
            new.append(outer)
        if after_pair is not None:
            after_pair(p)
        return tuple(new)

    start = max(2 * first - 1, 0)
    init = []
    for c in range(ext // 8):
        a, b = e[start, 8 + 8 * c : 16 + 8 * c, :], e[2 * first, 8 + 8 * c : 16 + 8 * c, :]
        init.append(a * b / (a + b))
    init = tuple(init)
    lax.fori_loop(first, last, body, init)


def clear(v, ext):
    def body(p, carry):
        for j in range(4):
            for k in range(2):
                v[k, 4 * p + j] = jnp.zeros((ext + 16, LANES), F32)
        return carry

    lax.fori_loop(0, ext // 8, body, 0)


def updated(level, k, p, v, state, low, high, base=(0, 0)):
    step = 1 << level
    even = pair_is_even(level, high - low)
    mid = slice(8 + low, 8 + high)
    other = 1 - k
    here = v[other, p, mid, :]
    before = v[other, p - 1, mid, :]
    after = v[other, p + 1, mid, :]
    outer = jnp.where(even, before, after) if k == 0 else jnp.where(even, after, before)
    rows = slice(low - base[1], high - base[1])
    part = [state[p - base[0], k, 1 + i, rows, :] for i in range(6)]
    x = part[0] * here + part[1] * outer
    y = part[2] * v[other, p, 9 + low : 9 + high, :] + part[3] * v[other, p, 7 + low : 7 + high, :]
    z = part[4] * lane_roll(here, -step) + part[5] * lane_roll(here, step)
    return (state[p - base[0], k, 0, rows, :] + x) + (y + z)


def half_sweep(level, k, reach, v, state, base=(0, 0)):
    own, halo, ext = OWN[level], HALO[level], EXT[level]
    first = (halo - reach) // 2
    last = (halo + own + reach + 1) // 2
    low = (halo - reach) // 8 * 8
    high = -(-(halo + own + reach) // 8) * 8

    def body(p):
        value = updated(level, k, p, v, state, low, high, base)

        def store():
            v[k, p, 8 + low : 8 + high, :] = value

        return store

    loop(first, last, body, UNROLL["sweep"])


def restrict(level, first, pairs, row, count, v, state, total, e, tmp, put):
    step = 1 << level
    low = row // 8 * 8
    high = -(-(row + 2 * count) // 8) * 8
    mid = slice(8 + low, 8 + high)

    def fine(q):
        p = first + q
        residual = (updated(level, 0, p, v, state, low, high) - v[0, p, mid, :]) * total[p, low:high, :]
        both = e[2 * p, mid, :] + e[2 * p + 1, mid, :]

        def store():
            tmp[0, q, low:high, :] = residual
            tmp[1, q, low:high, :] = both

        return store

    def coarse(q):
        out = []
        for i in range(2):
            a = tmp[i, q, pl.ds(row, count, stride=2), :] + tmp[i, q, pl.ds(row + 1, count, stride=2), :]
            out.append((a + flip(a, step)) * (0.125 if i else 0.25 * 0.25**level))
        return lambda: put(q, out[0], out[1])

    loop(0, pairs, fine, UNROLL["restrict"])
    loop(0, pairs, coarse, 2 * UNROLL["restrict"])


def interleave(f, e):
    return jnp.where((iota(f.shape, f.ndim - 1) & 1) == 0, f, e)


def split(both):
    low = (iota(both.shape, both.ndim - 1) & 1) == 0
    return jnp.where(low, both, lane_roll(both, 1)), jnp.where(low, lane_roll(both, -1), both)


def fill_rim(e, ext):
    e[ext : ext + 2] = jnp.ones((2, ext + 16, LANES), F32)
    e[0:ext, 0:8, :] = jnp.ones((ext, 8, LANES), F32)
    e[0:ext, 8 + ext :, :] = jnp.ones((ext, 8, LANES), F32)


def start_all(copies):
    for copy in copies:
        copy.start()


def wait_all(copies):
    for copy in copies:
        copy.wait()


def sweep_down(level, pairs, reaches, inner, e, f, state, v, total, tmp, gx, gy, put, after_pair=None):
    clamp_edges(level, e, gx, gy)
    prepare(level, pairs[0], pairs[1], e, f, state, total, v, gx, gy, after_pair)
    if STOP >= 2:
        half_sweep(level, 1, reaches[0], v, state)
        half_sweep(level, 0, reaches[1], v, state)
        half_sweep(level, 1, reaches[2], v, state)
    if STOP >= 3:
        restrict(level, *inner, v, state, total, e, tmp, put)


def down0(f_in, e_in, xl, xr, yl, yr, cl, cr, out, state, v, e, f, total, tmp, in_sems):
    gx, gy = lax.axis_index("gx"), lax.axis_index("gy")
    ya, yb = 0, 40
    copies = []
    for i, (target, own, off) in enumerate(((f, f_in, 0), (e, e_in, 8))):
        parts = (
            (xl.at[i], target.at[pl.ds(0, 8), pl.ds(off + 8, 32)]),
            (own, target.at[pl.ds(8, 32), pl.ds(off + 8, 32)]),
            (xr.at[i], target.at[pl.ds(40, 8), pl.ds(off + 8, 32)]),
            (yl.at[i], target.at[pl.ds(8, 32), pl.ds(off + ya, 8)]),
            (yr.at[i], target.at[pl.ds(8, 32), pl.ds(off + yb, 8)]),
            (cl.at[i, pl.ds(0, 8)], target.at[pl.ds(0, 8), pl.ds(off + ya, 8)]),
            (cl.at[i, pl.ds(8, 8)], target.at[pl.ds(40, 8), pl.ds(off + ya, 8)]),
            (cr.at[i, pl.ds(0, 8)], target.at[pl.ds(0, 8), pl.ds(off + yb, 8)]),
            (cr.at[i, pl.ds(8, 8)], target.at[pl.ds(40, 8), pl.ds(off + yb, 8)]),
        )
        for j, (source, to) in enumerate(parts):
            copies.append(pltpu.make_async_copy(source, to, in_sems.at[9 * i + j]))
    start_all(copies)
    fill_rim(e, 48)
    clear(v, 48)
    wait_all(copies)

    def put(q, fc, ec):
        out[q] = interleave(fc, ec)

    if STOP >= 1:
        sweep_down(0, (0, 24), (6, 5, 4), (4, 16, 8, 16), e, f, state, v, total, tmp, gx, gy, put)


def put_split(source, start, count, x, y, e, f):
    height = source.shape[1]

    def body(i):
        fi, ei = split(source[start + i])

        def store():
            f[x + i, pl.ds(y, height), :] = fi
            e[x + i, pl.ds(8 + y, height), :] = ei

        return store

    loop(0, count, body, UNROLL["put"])


def down1(own, xl, xr, yl, yr, out, kept, v, e, f, total, tmp, state, sems):
    gx, gy = lax.axis_index("gx"), lax.axis_index("gy")
    fill_rim(e, 48)
    clear(v, 48)
    put_split(xl, 0, 13, 3, 16, e, f)
    put_split(own, 0, 16, 16, 16, e, f)
    put_split(xr, 0, 13, 32, 16, e, f)
    put_split(yl, 0, 42, 3, 0, e, f)
    put_split(yr, 0, 42, 3, 32, e, f)

    def put(q, fc, ec):
        out[q] = interleave(fc, ec)

    first, last, low, high = KEPT
    copies = []
    for g in range(GROUPS):
        a = first + (last - first) * g // GROUPS
        b = first + (last - first) * (g + 1) // GROUPS
        copies.append((b - 1, pltpu.make_async_copy(
            state.at[pl.ds(a, b - a), :, :, pl.ds(low, high - low), :], kept.at[pl.ds(a - first, b - a)], sems.at[g])))

    def after_pair(p):
        for end, copy in copies:

            @pl.when(p == end)
            def _():
                copy.start()

    sweep_down(1, (2, 22), (11, 10, 9), (4, 16, 8, 16), e, f, state, v, total, tmp, gx, gy, put, after_pair)
    wait_all([copy for _, copy in copies])


def down2(own, xl, xr, yl, yr, out, state, v, e, f, total, tmp, coarse):
    gx, gy = lax.axis_index("gx"), lax.axis_index("gy")
    fill_rim(e, 32)
    clear(v, 32)
    put_split(xl, 0, 8, 0, 8, e, f)
    put_split(own, 0, 16, 8, 8, e, f)
    put_split(xr, 0, 8, 24, 8, e, f)
    put_split(yl, 0, 32, 0, 0, e, f)
    put_split(yr, 0, 32, 0, 24, e, f)

    def put(q, fc, ec):
        coarse[0, q, 0:4, :] = fc
        coarse[1, q, 0:4, :] = ec

    if STOP >= 1:
        sweep_down(2, (1, 15), (9, 8, 7), (6, 4, 12, 4), e, f, state, v, total, tmp, gx, gy, put)
    slot = iota((1, LANES), 1) & 7
    for i in range(2):
        for r in range(2):
            row = jnp.zeros((1, LANES), F32)
            for x1 in range(2):
                for y in range(4):
                    row = jnp.where(slot == 4 * x1 + y, coarse[i, 2 * x1 + r, y : y + 1, :], row)
            out[:, 2 * i + r : 2 * i + r + 1, :] = jnp.broadcast_to(row[None], (GX, 1, LANES))


BLOCK = (CHUNK, GX, LANES)


def pair_before(v, fill):
    axis = v.ndim - 2
    low = (iota(v.shape, v.ndim - 1) & 4) == 0
    moved = jnp.where(low, pltpu.roll(lane_roll(v, -4), 1, axis), lane_roll(v, 4))
    return jnp.where(low & (iota(v.shape, axis) == 0), fill, moved)


def pair_after(v, fill):
    axis = v.ndim - 2
    high = (iota(v.shape, v.ndim - 1) & 4) != 0
    moved = jnp.where(high, pltpu.roll(lane_roll(v, 4), GX - 1, axis), lane_roll(v, -4))
    return jnp.where(high & (iota(v.shape, axis) == GX - 1), fill, moved)


def y_after(level, v, following):
    lane = iota(v.shape, v.ndim - 1)
    if level == 3:
        return jnp.where((lane & 3) == 3, lane_roll(following, 3), lane_roll(v, -1))
    return jnp.where((lane & 2) == 2, lane_roll(following, 2), lane_roll(v, -2))


def y_before(level, v, preceding):
    lane = iota(v.shape, v.ndim - 1)
    if level == 3:
        return jnp.where((lane & 3) == 0, lane_roll(preceding, -3), lane_roll(v, 1))
    return jnp.where((lane & 2) == 0, lane_roll(preceding, -2), lane_roll(v, 2))


def slots(shape):
    lane = iota(shape, len(shape) - 1)
    return (lane & 1) | ((lane >> 2) & 2)


def tiles_from_slots(parts):
    slot = slots(parts[0].shape)
    return jnp.where(slot == 0, parts[0], jnp.where(slot == 1, parts[1], jnp.where(slot == 2, parts[2], parts[3])))


def slot_after(v, fill):
    slot = slots(v.shape)
    return jnp.where(slot == 3, fill, jnp.where(slot == 1, lane_roll(v, -7), lane_roll(v, -1)))


def slot_before(v, fill):
    slot = slots(v.shape)
    return jnp.where(slot == 0, fill, jnp.where(slot == 2, lane_roll(v, 7), lane_roll(v, 1)))


def coarse_levels(f3, e3, s3, w3, v3, s4):
    lane = iota((C3, GX, LANES), 2)
    even3 = ((lane ^ (lane >> 3)) & 1) == 0
    z_last3 = (lane >> 3) == 15
    chunks = range(0, GY, C3)

    def face(scale, a, b):
        return (2.0 * scale) * a * b / (a + b)

    zero = jnp.zeros((GX, LANES), F32)
    for k in range(2):
        e3[k, 0] = lane_roll(e3[k, 1], 3)
        e3[k, 1 + GY] = lane_roll(e3[k, GY], -3)
        v3[k, 0] = zero
        v3[k, 1 + GY] = zero
    scale = 0.25**3
    e4 = []
    for g in chunks:
        here = pl.ds(1 + g, C3)
        both = (e3[0, here], e3[1, here])
        inner = face(scale, both[0], both[1])
        outer = (face(scale, both[0], pair_before(both[1], both[0])),
                 face(scale, both[1], pair_after(both[0], both[1])))
        yp, ym, zp, zm, f = [], [], [], [], []
        for r in range(2):
            own = both[r]
            yp.append(face(scale, own, y_after(3, own, e3[r, pl.ds(2 + g, C3)])))
            ym.append(face(scale, own, y_before(3, own, e3[r, pl.ds(g, C3)])))
            z = jnp.where(z_last3, 0.0, face(scale, own, lane_roll(own, -8)))
            zp.append(z)
            zm.append(lane_roll(z, 8))
            f.append(f3[r, pl.ds(g, C3)])
        for k in range(2):
            a, b = k, 1 - k
            parts = [jnp.where(even3, t[a], t[b]) for t in (outer, yp, ym, zp, zm)]
            weight_sum = inner
            for t in parts:
                weight_sum = weight_sum + t
            inverse = 1.0 / weight_sum
            source = jnp.where(even3, f[a], f[b]) * inverse
            s3[k, 0, pl.ds(g, C3)] = source
            s3[k, 1, pl.ds(g, C3)] = inner * inverse
            for i in range(5):
                s3[k, 2 + i, pl.ds(g, C3)] = parts[i] * inverse
            if k == 0:
                w3[pl.ds(g, C3)] = weight_sum
                v3[0, here] = source
        t = both[0] + both[1]
        t = t + flip(t, 1)
        e4.append((t + flip(t, 8)) * 0.125)

    def update3(k, g):
        o = 1 - k
        own = v3[o, pl.ds(1 + g, C3)]
        before, after = pair_before(own, 0.0), pair_after(own, 0.0)
        outer = jnp.where(even3, before, after) if k == 0 else jnp.where(even3, after, before)
        sides = (own, outer, y_after(3, own, v3[o, pl.ds(2 + g, C3)]),
                 y_before(3, own, v3[o, pl.ds(g, C3)]), lane_roll(own, -8), lane_roll(own, 8))
        part = [s3[k, 1 + i, pl.ds(g, C3)] * sides[i] for i in range(6)]
        return ((s3[k, 0, pl.ds(g, C3)] + part[0]) + (part[1] + part[2])) + ((part[3] + part[4]) + part[5])

    def sweep3(k):
        for g in chunks:
            v3[k, pl.ds(1 + g, C3)] = update3(k, g)

    sweep3(1)
    sweep3(0)
    sweep3(1)
    f4 = []
    for g in chunks:
        t = (update3(0, g) - v3[0, pl.ds(1 + g, C3)]) * w3[pl.ds(g, C3)]
        t = t + flip(t, 1)
        f4.append((t + flip(t, 8)) * 0.125)

    def regroup(parts):
        tiles = [part[i] for part in parts for i in range(C3)]
        return [tiles_from_slots(tiles[b::CHUNK]) for b in range(CHUNK)]

    e4, f4 = regroup(e4), regroup(f4)
    tile = (GX, LANES)
    lane = iota(tile, 1)
    even4 = (((lane >> 1) ^ (lane >> 2) ^ (lane >> 4)) & 1) == 0
    z_last4 = (lane >> 4) == 7
    scale = 0.25**4
    e_after = e4[1:] + [slot_after(e4[0], lane_roll(e4[-1], -2))]
    e_before = [slot_before(e4[-1], lane_roll(e4[0], 2))] + e4[:-1]
    v = []
    for b in range(CHUNK):
        own = e4[b]
        z = jnp.where(z_last4, 0.0, face(scale, own, lane_roll(own, -16)))
        parts = [face(scale, own, pair_before(own, own)), face(scale, own, pair_after(own, own)),
                 face(scale, own, y_after(4, own, e_after[b])), face(scale, own, y_before(4, own, e_before[b])),
                 z, lane_roll(z, 16)]
        weight_sum = parts[0]
        for t in parts[1:]:
            weight_sum = weight_sum + t
        inverse = 1.0 / weight_sum
        source = f4[b] * inverse
        s4[0, b] = source
        for i in range(6):
            s4[1 + i, b] = parts[i] * inverse
        v.append(jnp.where(even4, source, 0.0))

    def sweep4(k, v):
        v = list(v)
        after = v[1:] + [slot_after(v[0], 0.0)]
        before = [slot_before(v[-1], 0.0)] + v[:-1]
        new = []
        for b in range(CHUNK):
            own = v[b]
            x = s4[1, b] * pair_before(own, 0.0) + s4[2, b] * pair_after(own, 0.0)
            y = s4[3, b] * y_after(4, own, after[b]) + s4[4, b] * y_before(4, own, before[b])
            z = s4[5, b] * lane_roll(own, -16) + s4[6, b] * lane_roll(own, 16)
            value = (s4[0, b] + z) + (x + y)
            new.append(jnp.where(even4, value, own) if k == 0 else jnp.where(even4, own, value))
        return tuple(new)

    v = sweep4(1, v)
    if STOP >= 11:
        v = lax.fori_loop(0, COARSE_SWEEPS - 1, lambda i, v: sweep4(1, sweep4(0, v)), v)
    slot = slots(tile)
    for a in range(GY // CHUNK):
        for b in range(CHUNK):
            u = jnp.where(slot == a, v[b], 0.0)
            u = u + flip(u, 1)
            u = u + flip(u, 8)
            g = 1 + CHUNK * a + b
            v3[0, g] = v3[0, g] + u
            v3[1, g] = v3[1, g] + u
    if STOP < 12:
        return
    sweep3(0)
    sweep3(1)
    sweep3(0)
    sweep3(1)


def around_from_level3(v3, up, gx, gy):
    shape = (GX, LANES)
    lane, sub = iota(shape, 1), iota(shape, 0)
    even3 = ((lane ^ (lane >> 3)) & 1) == 0
    head = (lane & 7) == 0
    outside = ((sub == 0) & (gx == 0)) | ((sub == 2) & (gx == GX - 1))
    up[...] = jnp.zeros(up.shape, F32)
    for dy in range(3):
        red = v3[0, gy + dy]
        black = v3[1, gy + dy]
        for r in range(2):
            t = jnp.where(even3, red, black) if r == 0 else jnp.where(even3, black, red)
            t = jnp.where(outside, 0.0, pltpu.roll(t, lax.rem(GX + 1 - gx, GX), 0))
            for s in range(8):
                w = jnp.where(head, lane_roll(t, -s), 0.0)
                w = w + lane_roll(w, 1)
                w = w + lane_roll(w, 2)
                w = w + lane_roll(w, 4)
                for dx in range(3):
                    x = 4 * dx + 2 * (s // 4) + r
                    y = 4 + 2 * (4 * dy + s % 4)
                    up[x, y : y + 2, :] = jnp.broadcast_to(w[dx : dx + 1], (2, LANES))


def climb(near, far, s0, i0, s1, i1, s2, i2, out, f3, e3, s3, w3, v3, s4, v2, v1, v0,
          up3, up):
    gx, gy = lax.axis_index("gx"), lax.axis_index("gy")
    clear(v2, 32)
    clear(v1, 48)
    clear(v0, 48)
    for c, held in enumerate((near, far)):
        for dx in range(4):
            for dy in range(4):
                g = (((gy // 8 + dx) & 3) * 4 + ((gy // 2 + dy) & 3)) * 2 + (gy & 1 if c == 0 else 1 - (gy & 1))
                for r in range(2):
                    f3[r, g] = held[dx, dy, pl.ds(r, GX, stride=4), :]
                    e3[r, 1 + g] = held[dx, dy, pl.ds(2 + r, GX, stride=4), :]
    if STOP >= 10:
        coarse_levels(f3, e3, s3, w3, v3, s4)
    around_from_level3(v3, up3, gx, gy)

    if STOP >= 13:

        def add2(p):
            new = [i2[k, p, 8:40, :] + up3[p - 2] for k in range(2)]

            def store():
                for k in range(2):
                    v2[k, p, 8:40, :] = new[k]

            return store

        loop(2, 14, add2, UNROLL["add"])
        half_sweep(2, 0, 6, v2, s2)
        half_sweep(2, 1, 5, v2, s2)
        half_sweep(2, 0, 4, v2, s2)
        half_sweep(2, 1, 3, v2, s2)

    def raised(level, first, last, offset, coarse_v, v_in, v):
        def doubled(c):
            rows = 24
            even = pair_is_even(level + 1, rows)
            start = 8 + (12 if level == 0 else 4)
            red = coarse_v[0, c, start : start + rows, :]
            black = coarse_v[1, c, start : start + rows, :]
            both = (jnp.where(even, red, black), jnp.where(even, black, red))

            def store():
                for s in range(2):
                    for twice in range(2):
                        up[c, s, pl.ds(twice, rows, stride=2), :] = both[s]

            return store

        loop(first, last, doubled, 2)

        def add(c):
            new = [(k, 2 * c - offset + s, v_in[k, 2 * c - offset + s, 8:56, :] + up[c, s])
                   for s in range(2) for k in range(2)]

            def store():
                for k, p, value in new:
                    v[k, p, 8:56, :] = value

            return store

        loop(first, last, add, 1)

    if STOP >= 14:
        raised(1, 4, 12, 4, v2, i1, v1)
        half_sweep(1, 0, 5, v1, s1, (KEPT[0], KEPT[2]))
        half_sweep(1, 1, 4, v1, s1, (KEPT[0], KEPT[2]))
        half_sweep(1, 0, 3, v1, s1, (KEPT[0], KEPT[2]))
        half_sweep(1, 1, 2, v1, s1, (KEPT[0], KEPT[2]))

    if STOP >= 15:
        raised(0, 7, 17, 12, v1, i0, v0)
        half_sweep(0, 0, 3, v0, s0)
        half_sweep(0, 1, 2, v0, s0)
        half_sweep(0, 0, 1, v0, s0)
        half_sweep(0, 1, 0, v0, s0)
    even = pair_is_even(0, 32)

    def finish(q):
        red = v0[0, 4 + q, 16:48, :]
        black = v0[1, 4 + q, 16:48, :]

        def store():
            out[2 * q] = jnp.where(even, red, black)
            out[2 * q + 1] = jnp.where(even, black, red)

        return store

    loop(0, 16, finish, 4)


def shaped(*dims):
    return jax.ShapeDtypeStruct(dims, F32)


def kept_shapes(level):
    ext = EXT[level]
    kept = shaped(ext // 2, 2, 7, ext, LANES)
    if level == 1:
        kept = shaped(KEPT[1] - KEPT[0], 2, 7, KEPT[3] - KEPT[2], LANES)
    return kept, shaped(2, ext // 2, ext + 16, LANES)


def down_scratch(level):
    ext = EXT[level]
    vmem = [(ext + 2, ext + 16, LANES), (ext, ext, LANES), (ext // 2, ext, LANES), (2, 16, ext, LANES)]
    return [pltpu.VMEM(s, F32) for s in vmem]


def kernel_call(body, in_spaces, out_shape, out_spaces, scratch, mib, *operands):
    def specs(spaces):
        return [pl.BlockSpec(memory_space=pltpu.VMEM if s == "v" else pl.ANY) for s in spaces]

    return pl.pallas_call(
        body,
        in_specs=specs(in_spaces),
        out_specs=tuple(specs(out_spaces)),
        out_shape=tuple(out_shape),
        scratch_shapes=scratch,
        compiler_params=pltpu.CompilerParams(vmem_limit_bytes=mib << 20),
        name=body.__name__,
    )(*operands)


def exchange(axis, to_next, to_previous):
    count = lax.axis_size(axis)
    onward = [(i, (i + 1) % count) for i in range(count)]
    backward = [((i + 1) % count, i) for i in range(count)]
    return lax.ppermute(to_next, axis, onward), lax.ppermute(to_previous, axis, backward)


def from_offset(values, dx, dy, dc):
    moves = []
    for g in range(GY):
        x, y, c = g // 8, (g // 2) % 4, g % 2
        moves.append((((x + dx) % 4 * 4 + (y + dy) % 4) * 2 + (c ^ dc), g))
    return lax.ppermute(values, "gy", moves)


def per_device(right_side, permittivity):
    both = (right_side, permittivity)
    xl, xr = exchange("gx", jnp.stack([b[24:] for b in both]), jnp.stack([b[:8] for b in both]))
    yl, yr = exchange("gy", jnp.stack([b[:, 24:] for b in both]), jnp.stack([b[:, :8] for b in both]))
    corners = jnp.concatenate([xl, xr], axis=1)
    cl, cr = exchange("gy", corners[:, :, 24:], corners[:, :, :8])
    p1, s0, v0 = kernel_call(
        down0, "aavvvvvv", (shaped(16, 16, LANES),) + kept_shapes(0), KEPT_SPEC,
        down_scratch(0) + [pltpu.SemaphoreType.DMA((18,))], 8,
        right_side, permittivity, xl, xr, yl, yr, cl, cr)

    xl, xr = exchange("gx", p1[3:], p1[:13])
    wide = jnp.concatenate([xl, p1, xr], axis=0)
    yl, yr = exchange("gy", wide, wide)
    p2, s1, v1 = kernel_call(
        down1, "vvvvv", (shaped(16, 16, LANES),) + kept_shapes(1), "vav", down_scratch(1)
        + [pltpu.VMEM((EXT[1] // 2, 2, 7, EXT[1], LANES), F32), pltpu.SemaphoreType.DMA((GROUPS,))], 16,
        p1, xl, xr, yl, yr)

    xl, xr = exchange("gx", p2[:8], p2[8:])
    wide = jnp.concatenate([xl, p2, xr], axis=0)
    yl, yr = exchange("gy", wide[:, :8], wide[:, 8:])
    p3, s2, v2 = kernel_call(
        down2, "vvvvv", (shaped(GX, 4, LANES),) + kept_shapes(2), KEPT_SPEC,
        down_scratch(2) + [pltpu.VMEM((2, 4, 8, LANES), F32)], 8, p2, xl, xr, yl, yr)

    column = lax.all_to_all(p3, "gx", 0, 0, tiled=True).reshape(4 * GX, LANES)
    along_y = jnp.stack([column] + [from_offset(column, 0, d, 0) for d in (1, 2, 3)])
    near = jnp.stack([along_y] + [from_offset(along_y, d, 0, 0) for d in (1, 2, 3)])
    far = from_offset(near, 0, 0, 1)
    return climb_call(near, far, s0, v0, s1, v1, s2, v2)


def climb_call(*operands):
    rows = GY + 2
    vmem = [
        (2, GY, GX, LANES), (2, rows, GX, LANES), (2, 7, GY, GX, LANES), (GY, GX, LANES), (2, rows, GX, LANES),
        (7, CHUNK, GX, LANES),
        (2, 16, 48, LANES), (2, 24, 64, LANES), (2, 24, 64, LANES), (12, 32, LANES), (17, 2, 48, LANES),
    ]
    scratch = [pltpu.VMEM(s, F32) for s in vmem]
    return kernel_call(climb, "vvvvvvvv", (shaped(32, 32, LANES),), "v", scratch, 14, *operands)[0]


def solution(mesh):
    placed = (P("gx", "gy", None), P("gx", "gy", None))
    return jax.shard_map(
        per_device, mesh=mesh, in_specs=placed, out_specs=P("gx", "gy", None), check_vma=False
    )
```

```python
import jax
import jax.numpy as jnp
from jax import lax
from jax.experimental import pallas as pl
from jax.experimental.pallas import tpu as pltpu
from jax.sharding import PartitionSpec as P

F32 = jnp.float32
LANES = 128
COARSE_SWEEPS = 12
OWN = (32, 16, 8)
HALO = (8, 16, 12)
EXT = (48, 48, 32)
GX = 8
GY = 32
CHUNK = 8
C3 = 16
KEPT = (5, 19, 8, 40)
GROUPS = 4


UNROLL = {"sweep": 8, "restrict": 4, "put": 16, "add": 4}
STOP = 99
KEPT_SPEC = "vvv"


def loop(first, last, body, step):
    def several(base, count):
        for store in [body(base + j) for j in range(count)]:
            store()

    whole = (last - first) // step
    if whole > 1:
        def one(i, carry):
            several(first + i * step, step)
            return carry

        lax.fori_loop(0, whole, one, 0)
    elif whole == 1:
        several(first, step)
    if (last - first) % step:
        several(first + whole * step, (last - first) % step)


def iota(shape, dim):
    return lax.broadcasted_iota(jnp.int32, shape, dim)


def lane_roll(v, shift):
    return pltpu.roll(v, shift % LANES, v.ndim - 1)


def flip(v, bit):
    lane = iota(v.shape, v.ndim - 1)
    return jnp.where((lane & bit) == 0, lane_roll(v, -bit), lane_roll(v, bit))


def pair_is_even(level, rows):
    shape = (rows, LANES)
    return ((iota(shape, 0) ^ (iota(shape, 1) >> level)) & 1) == 0


def bounds(level, index, count):
    own, halo, ext = OWN[level], HALO[level], EXT[level]
    low = halo - index * own
    high = halo + (count - index) * own
    return low, high


def clamp_edges(level, e, gx, gy):
    own, halo, ext = OWN[level], HALO[level], EXT[level]
    for back in range(-(-halo // own)):
        low = halo - back * own
        high = halo + own + back * own
        if low >= 1:

            @pl.when(gx == back)
            def _():
                e[low - 1] = e[low]

            @pl.when(gy == back)
            def _():
                e[0:ext, 8 + low - 1 : 8 + low, :] = e[0:ext, 8 + low : 8 + low + 1, :]

        if high < ext:

            @pl.when(gx == GX - 1 - back)
            def _():
                e[high] = e[high - 1]

            @pl.when(gy == GY - 1 - back)
            def _():
                e[0:ext, 8 + high : 8 + high + 1, :] = e[0:ext, 8 + high - 1 : 8 + high, :]


def faces(pairs):
    sums = [a + b for a, b in pairs]
    first = sums[0] * sums[1]
    whole = 1.0 / (first * sums[2])
    rest = whole * sums[2]
    inverse = (rest * sums[1], rest * sums[0], whole * first)
    return [a * b * i for (a, b), i in zip(pairs, inverse)]


def inverses(a, b):
    whole = 1.0 / (a * b)
    return whole * b, whole * a


def prepare(level, first, last, e, f, state, total, v, gx, gy, after_pair=None):
    ext = EXT[level]
    step = 1 << level
    source_scale = 0.5 * 4.0**level

    xlow, xhigh = bounds(level, gx, GX)
    ylow, yhigh = bounds(level, gy, GY)
    shape = (8, LANES)
    lane = iota(shape, 1)
    z_last = (lane >> level) == (LANES >> level) - 1
    even = pair_is_even(level, 8)
    aligned = all((HALO[level] + i * OWN[level]) % 8 == 0 for i in range(2))

    def tile(p, r, before, below):
        mid = slice(8 + r, 16 + r)
        up = slice(9 + r, 17 + r)
        e0 = e[2 * p, mid, :]
        e1 = e[2 * p + 1, mid, :]
        after = e[2 * p + 2, mid, :]
        outer0 = before
        inner, outer1, yp0 = faces(((e0, e1), (e1, after), (e0, e[2 * p, up, :])))
        yp1, zp0, zp1 = faces(((e1, e[2 * p + 1, up, :]), (e0, lane_roll(e0, -step)), (e1, lane_roll(e1, -step))))
        zp0 = jnp.where(z_last, 0.0, zp0)
        zp1 = jnp.where(z_last, 0.0, zp1)
        turned = pltpu.roll(yp0, 1, 0), pltpu.roll(yp1, 1, 0)
        if below is None:
            below = turned
        ym0, ym1 = (jnp.where(top, below[i], turned[i]) for i in range(2))
        zm0 = lane_roll(zp0, step)
        zm1 = lane_roll(zp1, step)
        f0 = f[2 * p, r : r + 8, :]
        f1 = f[2 * p + 1, r : r + 8, :]
        ok = (2 * p >= xlow) & (2 * p < xhigh)
        if aligned:
            ok = jnp.where(ok & (r >= ylow) & (r < yhigh), 1.0, 0.0)
        else:
            row = r + iota(shape, 0)
            ok = jnp.where(ok, 1.0, 0.0) * jnp.where((row >= ylow) & (row < yhigh), 1.0, 0.0)
        sides, sums = [], []
        for k in range(2):
            pick = even if k == 0 else jnp.logical_not(even)
            side = [inner] + [jnp.where(pick, a, b) for a, b in (
                (outer0, outer1), (yp0, yp1), (ym0, ym1), (zp0, zp1), (zm0, zm1))]
            sides.append(side)
            sums.append((side[0] + side[1]) + (side[2] + side[3]) + (side[4] + side[5]))
        inverse = inverses(*sums)
        for k in range(2):
            scaled = inverse[k] * ok
            source = (jnp.where(even, f0, f1) if k == 0 else jnp.where(even, f1, f0)) * (scaled * source_scale)
            state[p, k, 0, r : r + 8, :] = source
            for i in range(6):
                state[p, k, 1 + i, r : r + 8, :] = sides[k][i] * scaled
            if k == 0:
                total[p, r : r + 8, :] = sums[0]
                v[0, p, mid, :] = source
        return outer1, turned

    top = iota(shape, 0) == 0

    def body(p, carry):
        new, turned = [], None
        for c in range(ext // 8):
            outer, turned = tile(p, 8 * c, carry[c], turned)
            new.append(outer)
        if after_pair is not None:
            after_pair(p)
        return tuple(new)

    start = max(2 * first - 1, 0)
    init = []
    for c in range(ext // 8):
        a, b = e[start, 8 + 8 * c : 16 + 8 * c, :], e[2 * first, 8 + 8 * c : 16 + 8 * c, :]
        init.append(a * b / (a + b))
    init = tuple(init)
    lax.fori_loop(first, last, body, init)


def clear(v, ext):
    def body(p, carry):
        for j in range(4):
            for k in range(2):
                v[k, 4 * p + j] = jnp.zeros((ext + 16, LANES), F32)
        return carry

    lax.fori_loop(0, ext // 8, body, 0)


def updated(level, k, p, v, state, low, high, base=(0, 0)):
    step = 1 << level
    even = pair_is_even(level, high - low)
    mid = slice(8 + low, 8 + high)
    other = 1 - k
    here = v[other, p, mid, :]
    before = v[other, p - 1, mid, :]
    after = v[other, p + 1, mid, :]
    outer = jnp.where(even, before, after) if k == 0 else jnp.where(even, after, before)
    rows = slice(low - base[1], high - base[1])
    part = [state[p - base[0], k, 1 + i, rows, :] for i in range(6)]
    x = part[0] * here + part[1] * outer
    y = part[2] * v[other, p, 9 + low : 9 + high, :] + part[3] * v[other, p, 7 + low : 7 + high, :]
    z = part[4] * lane_roll(here, -step) + part[5] * lane_roll(here, step)
    return (state[p - base[0], k, 0, rows, :] + x) + (y + z)


def half_sweep(level, k, reach, v, state, base=(0, 0)):
    own, halo, ext = OWN[level], HALO[level], EXT[level]
    first = (halo - reach) // 2
    last = (halo + own + reach + 1) // 2
    low = (halo - reach) // 8 * 8
    high = -(-(halo + own + reach) // 8) * 8

    def body(p):
        value = updated(level, k, p, v, state, low, high, base)

        def store():
            v[k, p, 8 + low : 8 + high, :] = value

        return store

    loop(first, last, body, UNROLL["sweep"])


def restrict(level, first, pairs, row, count, v, state, total, e, tmp, put):
    step = 1 << level
    low = row // 8 * 8
    high = -(-(row + 2 * count) // 8) * 8
    mid = slice(8 + low, 8 + high)

    def fine(q):
        p = first + q
        residual = (updated(level, 0, p, v, state, low, high) - v[0, p, mid, :]) * total[p, low:high, :]
        both = e[2 * p, mid, :] + e[2 * p + 1, mid, :]

        def store():
            tmp[0, q, low:high, :] = residual
            tmp[1, q, low:high, :] = both

        return store

    def coarse(q):
        out = []
        for i in range(2):
            a = tmp[i, q, pl.ds(row, count, stride=2), :] + tmp[i, q, pl.ds(row + 1, count, stride=2), :]
            out.append((a + flip(a, step)) * (0.125 if i else 0.25 * 0.25**level))
        return lambda: put(q, out[0], out[1])

    loop(0, pairs, fine, UNROLL["restrict"])
    loop(0, pairs, coarse, 2 * UNROLL["restrict"])


def interleave(f, e):
    return jnp.where((iota(f.shape, f.ndim - 1) & 1) == 0, f, e)


def split(both):
    low = (iota(both.shape, both.ndim - 1) & 1) == 0
    return jnp.where(low, both, lane_roll(both, 1)), jnp.where(low, lane_roll(both, -1), both)


def fill_rim(e, ext):
    e[ext : ext + 2] = jnp.ones((2, ext + 16, LANES), F32)
    e[0:ext, 0:8, :] = jnp.ones((ext, 8, LANES), F32)
    e[0:ext, 8 + ext :, :] = jnp.ones((ext, 8, LANES), F32)


def start_all(copies):
    for copy in copies:
        copy.start()


def wait_all(copies):
    for copy in copies:
        copy.wait()


def sweep_down(level, pairs, reaches, inner, e, f, state, v, total, tmp, gx, gy, put, after_pair=None):
    clamp_edges(level, e, gx, gy)
    prepare(level, pairs[0], pairs[1], e, f, state, total, v, gx, gy, after_pair)
    if STOP >= 2:
        half_sweep(level, 1, reaches[0], v, state)
        half_sweep(level, 0, reaches[1], v, state)
        half_sweep(level, 1, reaches[2], v, state)
    if STOP >= 3:
        restrict(level, *inner, v, state, total, e, tmp, put)


def down0(f_in, e_in, xl, xr, yl, yr, cl, cr, out, state, v, e, f, total, tmp, in_sems):
    gx, gy = lax.axis_index("gx"), lax.axis_index("gy")
    ya, yb = 0, 40
    copies = []
    for i, (target, own, off) in enumerate(((f, f_in, 0), (e, e_in, 8))):
        parts = (
            (xl.at[i], target.at[pl.ds(0, 8), pl.ds(off + 8, 32)]),
            (own, target.at[pl.ds(8, 32), pl.ds(off + 8, 32)]),
            (xr.at[i], target.at[pl.ds(40, 8), pl.ds(off + 8, 32)]),
            (yl.at[i], target.at[pl.ds(8, 32), pl.ds(off + ya, 8)]),
            (yr.at[i], target.at[pl.ds(8, 32), pl.ds(off + yb, 8)]),
            (cl.at[i, pl.ds(0, 8)], target.at[pl.ds(0, 8), pl.ds(off + ya, 8)]),
            (cl.at[i, pl.ds(8, 8)], target.at[pl.ds(40, 8), pl.ds(off + ya, 8)]),
            (cr.at[i, pl.ds(0, 8)], target.at[pl.ds(0, 8), pl.ds(off + yb, 8)]),
            (cr.at[i, pl.ds(8, 8)], target.at[pl.ds(40, 8), pl.ds(off + yb, 8)]),
        )
        for j, (source, to) in enumerate(parts):
            copies.append(pltpu.make_async_copy(source, to, in_sems.at[9 * i + j]))
    start_all(copies)
    fill_rim(e, 48)
    clear(v, 48)
    wait_all(copies)

    def put(q, fc, ec):
        out[q] = interleave(fc, ec)

    if STOP >= 1:
        sweep_down(0, (0, 24), (6, 5, 4), (4, 16, 8, 16), e, f, state, v, total, tmp, gx, gy, put)


def put_split(source, start, count, x, y, e, f):
    height = source.shape[1]

    def body(i):
        fi, ei = split(source[start + i])

        def store():
            f[x + i, pl.ds(y, height), :] = fi
            e[x + i, pl.ds(8 + y, height), :] = ei

        return store

    loop(0, count, body, UNROLL["put"])


def down1(own, xl, xr, yl, yr, out, kept, v, e, f, total, tmp, state, sems):
    gx, gy = lax.axis_index("gx"), lax.axis_index("gy")
    fill_rim(e, 48)
    clear(v, 48)
    put_split(xl, 0, 13, 3, 16, e, f)
    put_split(own, 0, 16, 16, 16, e, f)
    put_split(xr, 0, 13, 32, 16, e, f)
    put_split(yl, 0, 42, 3, 0, e, f)
    put_split(yr, 0, 42, 3, 32, e, f)

    def put(q, fc, ec):
        out[q] = interleave(fc, ec)

    first, last, low, high = KEPT
    copies = []
    for g in range(GROUPS):
        a = first + (last - first) * g // GROUPS
        b = first + (last - first) * (g + 1) // GROUPS
        copies.append((b - 1, pltpu.make_async_copy(
            state.at[pl.ds(a, b - a), :, :, pl.ds(low, high - low), :], kept.at[pl.ds(a - first, b - a)], sems.at[g])))

    def after_pair(p):
        for end, copy in copies:

            @pl.when(p == end)
            def _():
                copy.start()

    sweep_down(1, (2, 22), (11, 10, 9), (4, 16, 8, 16), e, f, state, v, total, tmp, gx, gy, put, after_pair)
    wait_all([copy for _, copy in copies])


def down2(own, xl, xr, yl, yr, out, state, v, e, f, total, tmp, coarse):
    gx, gy = lax.axis_index("gx"), lax.axis_index("gy")
    fill_rim(e, 32)
    clear(v, 32)
    put_split(xl, 0, 8, 0, 8, e, f)
    put_split(own, 0, 16, 8, 8, e, f)
    put_split(xr, 0, 8, 24, 8, e, f)
    put_split(yl, 0, 32, 0, 0, e, f)
    put_split(yr, 0, 32, 0, 24, e, f)

    def put(q, fc, ec):
        coarse[0, q, 0:4, :] = fc
        coarse[1, q, 0:4, :] = ec

    if STOP >= 1:
        sweep_down(2, (1, 15), (9, 8, 7), (6, 4, 12, 4), e, f, state, v, total, tmp, gx, gy, put)
    slot = iota((1, LANES), 1) & 7
    for i in range(2):
        for r in range(2):
            row = jnp.zeros((1, LANES), F32)
            for x1 in range(2):
                for y in range(4):
                    row = jnp.where(slot == 4 * x1 + y, coarse[i, 2 * x1 + r, y : y + 1, :], row)
            out[:, 2 * i + r : 2 * i + r + 1, :] = jnp.broadcast_to(row[None], (GX, 1, LANES))


BLOCK = (CHUNK, GX, LANES)


def pair_before(v, fill):
    axis = v.ndim - 2
    low = (iota(v.shape, v.ndim - 1) & 4) == 0
    moved = jnp.where(low, pltpu.roll(lane_roll(v, -4), 1, axis), lane_roll(v, 4))
    return jnp.where(low & (iota(v.shape, axis) == 0), fill, moved)


def pair_after(v, fill):
    axis = v.ndim - 2
    high = (iota(v.shape, v.ndim - 1) & 4) != 0
    moved = jnp.where(high, pltpu.roll(lane_roll(v, 4), GX - 1, axis), lane_roll(v, -4))
    return jnp.where(high & (iota(v.shape, axis) == GX - 1), fill, moved)


def y_after(level, v, following):
    lane = iota(v.shape, v.ndim - 1)
    if level == 3:
        return jnp.where((lane & 3) == 3, lane_roll(following, 3), lane_roll(v, -1))
    return jnp.where((lane & 2) == 2, lane_roll(following, 2), lane_roll(v, -2))


def y_before(level, v, preceding):
    lane = iota(v.shape, v.ndim - 1)
    if level == 3:
        return jnp.where((lane & 3) == 0, lane_roll(preceding, -3), lane_roll(v, 1))
    return jnp.where((lane & 2) == 0, lane_roll(preceding, -2), lane_roll(v, 2))


def slots(shape):
    lane = iota(shape, len(shape) - 1)
    return (lane & 1) | ((lane >> 2) & 2)


def tiles_from_slots(parts):
    slot = slots(parts[0].shape)
    return jnp.where(slot == 0, parts[0], jnp.where(slot == 1, parts[1], jnp.where(slot == 2, parts[2], parts[3])))


def slot_after(v, fill):
    slot = slots(v.shape)
    return jnp.where(slot == 3, fill, jnp.where(slot == 1, lane_roll(v, -7), lane_roll(v, -1)))


def slot_before(v, fill):
    slot = slots(v.shape)
    return jnp.where(slot == 0, fill, jnp.where(slot == 2, lane_roll(v, 7), lane_roll(v, 1)))


def coarse_levels(f3, e3, s3, w3, v3, s4):
    lane = iota((C3, GX, LANES), 2)
    even3 = ((lane ^ (lane >> 3)) & 1) == 0
    z_last3 = (lane >> 3) == 15
    chunks = range(0, GY, C3)

    def face(scale, a, b):
        return (2.0 * scale) * a * b / (a + b)

    zero = jnp.zeros((GX, LANES), F32)
    for k in range(2):
        e3[k, 0] = lane_roll(e3[k, 1], 3)
        e3[k, 1 + GY] = lane_roll(e3[k, GY], -3)
        v3[k, 0] = zero
        v3[k, 1 + GY] = zero
    scale = 0.25**3
    e4 = []
    for g in chunks:
        here = pl.ds(1 + g, C3)
        both = (e3[0, here], e3[1, here])
        inner = face(scale, both[0], both[1])
        outer = (face(scale, both[0], pair_before(both[1], both[0])),
                 face(scale, both[1], pair_after(both[0], both[1])))
        yp, ym, zp, zm, f = [], [], [], [], []
        for r in range(2):
            own = both[r]
            yp.append(face(scale, own, y_after(3, own, e3[r, pl.ds(2 + g, C3)])))
            ym.append(face(scale, own, y_before(3, own, e3[r, pl.ds(g, C3)])))
            z = jnp.where(z_last3, 0.0, face(scale, own, lane_roll(own, -8)))
            zp.append(z)
            zm.append(lane_roll(z, 8))
            f.append(f3[r, pl.ds(g, C3)])
        for k in range(2):
            a, b = k, 1 - k
            parts = [jnp.where(even3, t[a], t[b]) for t in (outer, yp, ym, zp, zm)]
            weight_sum = inner
            for t in parts:
                weight_sum = weight_sum + t
            inverse = 1.0 / weight_sum
            source = jnp.where(even3, f[a], f[b]) * inverse
            s3[k, 0, pl.ds(g, C3)] = source
            s3[k, 1, pl.ds(g, C3)] = inner * inverse
            for i in range(5):
                s3[k, 2 + i, pl.ds(g, C3)] = parts[i] * inverse
            if k == 0:
                w3[pl.ds(g, C3)] = weight_sum
                v3[0, here] = source
        t = both[0] + both[1]
        t = t + flip(t, 1)
        e4.append((t + flip(t, 8)) * 0.125)

    def update3(k, g):
        o = 1 - k
        own = v3[o, pl.ds(1 + g, C3)]
        before, after = pair_before(own, 0.0), pair_after(own, 0.0)
        outer = jnp.where(even3, before, after) if k == 0 else jnp.where(even3, after, before)
        sides = (own, outer, y_after(3, own, v3[o, pl.ds(2 + g, C3)]),
                 y_before(3, own, v3[o, pl.ds(g, C3)]), lane_roll(own, -8), lane_roll(own, 8))
        part = [s3[k, 1 + i, pl.ds(g, C3)] * sides[i] for i in range(6)]
        return ((s3[k, 0, pl.ds(g, C3)] + part[0]) + (part[1] + part[2])) + ((part[3] + part[4]) + part[5])

    def sweep3(k):
        for g in chunks:
            v3[k, pl.ds(1 + g, C3)] = update3(k, g)

    sweep3(1)
    sweep3(0)
    sweep3(1)
    f4 = []
    for g in chunks:
        t = (update3(0, g) - v3[0, pl.ds(1 + g, C3)]) * w3[pl.ds(g, C3)]
        t = t + flip(t, 1)
        f4.append((t + flip(t, 8)) * 0.125)

    def regroup(parts):
        tiles = [part[i] for part in parts for i in range(C3)]
        return [tiles_from_slots(tiles[b::CHUNK]) for b in range(CHUNK)]

    e4, f4 = regroup(e4), regroup(f4)
    tile = (GX, LANES)
    lane = iota(tile, 1)
    even4 = (((lane >> 1) ^ (lane >> 2) ^ (lane >> 4)) & 1) == 0
    z_last4 = (lane >> 4) == 7
    scale = 0.25**4
    e_after = e4[1:] + [slot_after(e4[0], lane_roll(e4[-1], -2))]
    e_before = [slot_before(e4[-1], lane_roll(e4[0], 2))] + e4[:-1]
    v = []
    for b in range(CHUNK):
        own = e4[b]
        z = jnp.where(z_last4, 0.0, face(scale, own, lane_roll(own, -16)))
        parts = [face(scale, own, pair_before(own, own)), face(scale, own, pair_after(own, own)),
                 face(scale, own, y_after(4, own, e_after[b])), face(scale, own, y_before(4, own, e_before[b])),
                 z, lane_roll(z, 16)]
        weight_sum = parts[0]
        for t in parts[1:]:
            weight_sum = weight_sum + t
        inverse = 1.0 / weight_sum
        source = f4[b] * inverse
        s4[0, b] = source
        for i in range(6):
            s4[1 + i, b] = parts[i] * inverse
        v.append(jnp.where(even4, source, 0.0))

    def sweep4(k, v):
        v = list(v)
        after = v[1:] + [slot_after(v[0], 0.0)]
        before = [slot_before(v[-1], 0.0)] + v[:-1]
        new = []
        for b in range(CHUNK):
            own = v[b]
            x = s4[1, b] * pair_before(own, 0.0) + s4[2, b] * pair_after(own, 0.0)
            y = s4[3, b] * y_after(4, own, after[b]) + s4[4, b] * y_before(4, own, before[b])
            z = s4[5, b] * lane_roll(own, -16) + s4[6, b] * lane_roll(own, 16)
            value = (s4[0, b] + z) + (x + y)
            new.append(jnp.where(even4, value, own) if k == 0 else jnp.where(even4, own, value))
        return tuple(new)

    v = sweep4(1, v)
    if STOP >= 11:
        v = lax.fori_loop(0, COARSE_SWEEPS - 1, lambda i, v: sweep4(1, sweep4(0, v)), v)
    slot = slots(tile)
    for a in range(GY // CHUNK):
        for b in range(CHUNK):
            u = jnp.where(slot == a, v[b], 0.0)
            u = u + flip(u, 1)
            u = u + flip(u, 8)
            g = 1 + CHUNK * a + b
            v3[0, g] = v3[0, g] + u
            v3[1, g] = v3[1, g] + u
    if STOP < 12:
        return
    sweep3(0)
    sweep3(1)
    sweep3(0)
    sweep3(1)


def around_from_level3(v3, up, gx, gy):
    shape = (GX, LANES)
    lane, sub = iota(shape, 1), iota(shape, 0)
    even3 = ((lane ^ (lane >> 3)) & 1) == 0
    head = (lane & 7) == 0
    outside = ((sub == 0) & (gx == 0)) | ((sub == 2) & (gx == GX - 1))
    up[...] = jnp.zeros(up.shape, F32)
    for dy in range(3):
        red = v3[0, gy + dy]
        black = v3[1, gy + dy]
        for r in range(2):
            t = jnp.where(even3, red, black) if r == 0 else jnp.where(even3, black, red)
            t = jnp.where(outside, 0.0, pltpu.roll(t, lax.rem(GX + 1 - gx, GX), 0))
            for s in range(8):
                w = jnp.where(head, lane_roll(t, -s), 0.0)
                w = w + lane_roll(w, 1)
                w = w + lane_roll(w, 2)
                w = w + lane_roll(w, 4)
                for dx in range(3):
                    x = 4 * dx + 2 * (s // 4) + r
                    y = 4 + 2 * (4 * dy + s % 4)
                    up[x, y : y + 2, :] = jnp.broadcast_to(w[dx : dx + 1], (2, LANES))


def climb(near, far, s0, i0, s1, i1, s2, i2, out, f3, e3, s3, w3, v3, s4, v2, v1, v0,
          up3, up):
    gx, gy = lax.axis_index("gx"), lax.axis_index("gy")
    clear(v2, 32)
    clear(v1, 48)
    clear(v0, 48)
    for c, held in enumerate((near, far)):
        for dx in range(4):
            for dy in range(4):
                g = (((gy // 8 + dx) & 3) * 4 + ((gy // 2 + dy) & 3)) * 2 + (gy & 1 if c == 0 else 1 - (gy & 1))
                for r in range(2):
                    f3[r, g] = held[dx, dy, pl.ds(r, GX, stride=4), :]
                    e3[r, 1 + g] = held[dx, dy, pl.ds(2 + r, GX, stride=4), :]
    if STOP >= 10:
        coarse_levels(f3, e3, s3, w3, v3, s4)
    around_from_level3(v3, up3, gx, gy)

    if STOP >= 13:

        def add2(p):
            new = [i2[k, p, 8:40, :] + up3[p - 2] for k in range(2)]

            def store():
                for k in range(2):
                    v2[k, p, 8:40, :] = new[k]

            return store

        loop(2, 14, add2, UNROLL["add"])
        half_sweep(2, 0, 6, v2, s2)
        half_sweep(2, 1, 5, v2, s2)
        half_sweep(2, 0, 4, v2, s2)
        half_sweep(2, 1, 3, v2, s2)

    def raised(level, first, last, offset, coarse_v, v_in, v):
        def doubled(c):
            rows = 24
            even = pair_is_even(level + 1, rows)
            start = 8 + (12 if level == 0 else 4)
            red = coarse_v[0, c, start : start + rows, :]
            black = coarse_v[1, c, start : start + rows, :]
            both = (jnp.where(even, red, black), jnp.where(even, black, red))

            def store():
                for s in range(2):
                    for twice in range(2):
                        up[c, s, pl.ds(twice, rows, stride=2), :] = both[s]

            return store

        loop(first, last, doubled, 2)

        def add(c):
            new = [(k, 2 * c - offset + s, v_in[k, 2 * c - offset + s, 8:56, :] + up[c, s])
                   for s in range(2) for k in range(2)]

            def store():
                for k, p, value in new:
                    v[k, p, 8:56, :] = value

            return store

        loop(first, last, add, 1)

    if STOP >= 14:
        raised(1, 4, 12, 4, v2, i1, v1)
        half_sweep(1, 0, 5, v1, s1, (KEPT[0], KEPT[2]))
        half_sweep(1, 1, 4, v1, s1, (KEPT[0], KEPT[2]))
        half_sweep(1, 0, 3, v1, s1, (KEPT[0], KEPT[2]))
        half_sweep(1, 1, 2, v1, s1, (KEPT[0], KEPT[2]))

    if STOP >= 15:
        raised(0, 7, 17, 12, v1, i0, v0)
        half_sweep(0, 0, 3, v0, s0)
        half_sweep(0, 1, 2, v0, s0)
        half_sweep(0, 0, 1, v0, s0)
        half_sweep(0, 1, 0, v0, s0)
    even = pair_is_even(0, 32)

    def finish(q):
        red = v0[0, 4 + q, 16:48, :]
        black = v0[1, 4 + q, 16:48, :]

        def store():
            out[2 * q] = jnp.where(even, red, black)
            out[2 * q + 1] = jnp.where(even, black, red)

        return store

    loop(0, 16, finish, 4)


def shaped(*dims):
    return jax.ShapeDtypeStruct(dims, F32)


def kept_shapes(level):
    ext = EXT[level]
    kept = shaped(ext // 2, 2, 7, ext, LANES)
    if level == 1:
        kept = shaped(KEPT[1] - KEPT[0], 2, 7, KEPT[3] - KEPT[2], LANES)
    return kept, shaped(2, ext // 2, ext + 16, LANES)


def down_scratch(level):
    ext = EXT[level]
    vmem = [(ext + 2, ext + 16, LANES), (ext, ext, LANES), (ext // 2, ext, LANES), (2, 16, ext, LANES)]
    return [pltpu.VMEM(s, F32) for s in vmem]


def kernel_call(body, in_spaces, out_shape, out_spaces, scratch, mib, *operands):
    def specs(spaces):
        return [pl.BlockSpec(memory_space=pltpu.VMEM if s == "v" else pl.ANY) for s in spaces]

    return pl.pallas_call(
        body,
        in_specs=specs(in_spaces),
        out_specs=tuple(specs(out_spaces)),
        out_shape=tuple(out_shape),
        scratch_shapes=scratch,
        compiler_params=pltpu.CompilerParams(vmem_limit_bytes=mib << 20),
        name=body.__name__,
    )(*operands)


def exchange(axis, to_next, to_previous):
    count = lax.axis_size(axis)
    onward = [(i, (i + 1) % count) for i in range(count)]
    backward = [((i + 1) % count, i) for i in range(count)]
    return lax.ppermute(to_next, axis, onward), lax.ppermute(to_previous, axis, backward)


def from_offset(values, dx, dy, dc):
    moves = []
    for g in range(GY):
        x, y, c = g // 8, (g // 2) % 4, g % 2
        moves.append((((x + dx) % 4 * 4 + (y + dy) % 4) * 2 + (c ^ dc), g))
    return lax.ppermute(values, "gy", moves)


def per_device(right_side, permittivity):
    both = (right_side, permittivity)
    xl, xr = exchange("gx", jnp.stack([b[24:] for b in both]), jnp.stack([b[:8] for b in both]))
    yl, yr = exchange("gy", jnp.stack([b[:, 24:] for b in both]), jnp.stack([b[:, :8] for b in both]))
    corners = jnp.concatenate([xl, xr], axis=1)
    cl, cr = exchange("gy", corners[:, :, 24:], corners[:, :, :8])
    p1, s0, v0 = kernel_call(
        down0, "aavvvvvv", (shaped(16, 16, LANES),) + kept_shapes(0), KEPT_SPEC,
        down_scratch(0) + [pltpu.SemaphoreType.DMA((18,))], 8,
        right_side, permittivity, xl, xr, yl, yr, cl, cr)

    xl, xr = exchange("gx", p1[3:], p1[:13])
    wide = jnp.concatenate([xl, p1, xr], axis=0)
    yl, yr = exchange("gy", wide, wide)
    p2, s1, v1 = kernel_call(
        down1, "vvvvv", (shaped(16, 16, LANES),) + kept_shapes(1), "vav", down_scratch(1)
        + [pltpu.VMEM((EXT[1] // 2, 2, 7, EXT[1], LANES), F32), pltpu.SemaphoreType.DMA((GROUPS,))], 16,
        p1, xl, xr, yl, yr)

    xl, xr = exchange("gx", p2[:8], p2[8:])
    wide = jnp.concatenate([xl, p2, xr], axis=0)
    yl, yr = exchange("gy", wide[:, :8], wide[:, 8:])
    p3, s2, v2 = kernel_call(
        down2, "vvvvv", (shaped(GX, 4, LANES),) + kept_shapes(2), KEPT_SPEC,
        down_scratch(2) + [pltpu.VMEM((2, 4, 8, LANES), F32)], 8, p2, xl, xr, yl, yr)

    column = lax.all_to_all(p3, "gx", 0, 0, tiled=True).reshape(4 * GX, LANES)
    along_y = jnp.stack([column] + [from_offset(column, 0, d, 0) for d in (1, 2, 3)])
    near = jnp.stack([along_y] + [from_offset(along_y, d, 0, 0) for d in (1, 2, 3)])
    far = from_offset(near, 0, 0, 1)
    return climb_call(near, far, s0, v0, s1, v1, s2, v2)


def climb_call(*operands):
    rows = GY + 2
    vmem = [
        (2, GY, GX, LANES), (2, rows, GX, LANES), (2, 7, GY, GX, LANES), (GY, GX, LANES), (2, rows, GX, LANES),
        (7, CHUNK, GX, LANES),
        (2, 16, 48, LANES), (2, 24, 64, LANES), (2, 24, 64, LANES), (12, 32, LANES), (17, 2, 48, LANES),
    ]
    scratch = [pltpu.VMEM(s, F32) for s in vmem]
    return kernel_call(climb, "vvvvvvvv", (shaped(32, 32, LANES),), "v", scratch, 14, *operands)[0]


def solution(mesh):
    placed = (P("gx", "gy", None), P("gx", "gy", None))
    return jax.shard_map(
        per_device, mesh=mesh, in_specs=placed, out_specs=P("gx", "gy", None), check_vma=False
    )
```
